32 devices in a mesh: expert: 8 (over z, y), tensor: 4 (over x, core).
Axes of the slice: x: 2, y: 2, z: 4, core: 2. Of those that a mesh axis runs over, the one named last changes fastest.
Arguments:
- layer_input: bfloat16 [4096, 2080], P(('expert', 'tensor'))
- residual: bfloat16 [4096, 2080], P(('expert', 'tensor'))
- out_grad: bfloat16 [4096, 2080], P(('expert', 'tensor')), may hold values from -6 to 6
- gate_prob: float32 [4096], P(('expert', 'tensor')), may hold values from 0.2 to 1
- expert_ids: int32 [4096], P(('expert', 'tensor')), may hold values from 0 to 7, as said below
- slot_index: int32 [4096], P(('expert', 'tensor')), may hold values from -1 to 19, as said below
- segment_ids: int32 [4096], P('expert'), may hold values from 0 to 3, as said below
- query_rows: bfloat16 [4096, 1024], P('expert', 'tensor'), may hold values from -6 to 6
- key_rows: bfloat16 [4096, 1024], P('expert', 'tensor'), may hold values from -6 to 6
- value_rows: bfloat16 [4096, 1024], P('expert', 'tensor'), may hold values from -6 to 6
- attn_heads: bfloat16 [4096, 1024], P('expert', 'tensor'), may hold values from -6 to 6
- attn_gain: float32 [2080], replicated, may hold values from 0.5 to 1.5
- expert_gain: float32 [2080], replicated, may hold values from 0.5 to 1.5
- query_weight: bfloat16 [2080, 1024], P(None, 'tensor'), may hold values from -0.125 to 0.125
- key_weight: bfloat16 [2080, 1024], P(None, 'tensor'), may hold values from -0.125 to 0.125
- value_weight: bfloat16 [2080, 1024], P(None, 'tensor'), may hold values from -0.125 to 0.125
- output_weight: bfloat16 [1024, 2080], P('tensor'), may hold values from -0.1875 to 0.1875
- inner_weight: bfloat16 [8, 2080, 3072], P('expert', None, 'tensor'), may hold values from -0.125 to 0.125
- outer_weight: bfloat16 [8, 3072, 2080], P('expert', 'tensor'), may hold values from -0.109375 to 0.109375
- hidden_pre: bfloat16 [8, 4, 8, 20, 3072], P('expert', None, None, None, 'tensor'), may hold values from -6 to 6
Outputs:
- input_grad: bfloat16 [4096, 2080], P(('expert', 'tensor'))
- attn_gain_grad: float32 [2080], replicated
- expert_gain_grad: float32 [2080], replicated
- query_grad: bfloat16 [2080, 1024], P('expert', 'tensor')
- key_grad: bfloat16 [2080, 1024], P('expert', 'tensor')
- value_grad: bfloat16 [2080, 1024], P('expert', 'tensor')
- output_grad: bfloat16 [1024, 2080], P('tensor', 'expert')
- inner_grad: bfloat16 [8, 2080, 3072], P('expert', None, 'tensor')
- outer_grad: bfloat16 [8, 3072, 2080], P('expert', 'tensor')
- gate_grad: bfloat16 [4096], P(('expert', 'tensor'))
The draws below stay inside these ranges and needn't reach their ends.
Inputs may be any that keep to these rules, and one draw needn't show every extreme that they name: `expert_ids`: in every device's 128 tokens, half name one expert, the same on every device and drawn from the seed; the others name experts evenly at random. `slot_index`: -1 marks a dropped token; otherwise the slot is the number of earlier tokens of the same device with the same expert, so at most 20 tokens of one device hold slots of one expert, and every device fills all 20 slots of the expert that half of its tokens name. `segment_ids`: every sequence of 512 tokens holds four documents: the ids start at 0, never fall and rise by one at each new document; every document has an even length and starts at an even position of its sequence; one document of each sequence holds more than half of its tokens.
All inputs are finite; a program needn't handle non-finite values.
Results may differ from the reference program's by a relative error of at most 0.023.
Values may be sent and summed in bfloat16 or wider, within the bound.
No kernel may reach another device: no remote copies, remote signals or barrier semaphores. Data moves between devices by JAX's collectives and lax.ppermute only.
A program may use at most 128 MiB of HBM per device.

```python
import jax
import jax.numpy as jnp
from jax import lax

D = 2080
HEADS = 16
DH = 64
FF = 3072
TOK_DEV = 128
HD = 1024
SEQ = 512
TOKENS = 4096
EXPERTS = 8
CAP = 20
N_EXPERT = 8
N_TENSOR = 4


def scaled_rows(key):
    base_key, column_key, row_key = jax.random.split(key, 3)
    columns = jnp.exp(jax.random.uniform(column_key, (1, D), minval=0.0, maxval=2.3))
    row_scale = jnp.exp(jax.random.uniform(row_key, (TOKENS, 1), minval=0.0, maxval=2.3))
    base = jax.random.normal(base_key, (TOKENS, D))
    return (jnp.clip(base, -4.0, 4.0) * columns * row_scale * 0.1).astype(jnp.bfloat16)


def draw_layer_input(key, part):
    return scaled_rows(jax.random.fold_in(key, 3))


def draw_residual(key, part):
    return scaled_rows(jax.random.fold_in(key, 4))


def routing(key):
    base_key, hot_key, order_key = jax.random.split(jax.random.fold_in(key, 7), 3)
    blocks = TOKENS // TOK_DEV
    chosen = jax.random.randint(base_key, (blocks, TOK_DEV), 0, EXPERTS)
    hot_expert = jax.random.randint(hot_key, (), 0, EXPERTS)
    orders = jax.vmap(lambda one_key: jax.random.permutation(one_key, TOK_DEV))(jax.random.split(order_key, blocks))
    ranks = jnp.argsort(orders, axis=1)
    chosen = jnp.where(ranks < TOK_DEV // 2, hot_expert, chosen)
    onehot = (chosen[:, :, None] == jnp.arange(EXPERTS, dtype=jnp.int32)[None, None, :]).astype(jnp.int32)
    before = jnp.cumsum(onehot, axis=1) - onehot
    order_in = jnp.sum(before * onehot, axis=2)
    slots = jnp.where(order_in < CAP, order_in, -1)
    return (chosen.reshape(TOKENS).astype(jnp.int32), slots.reshape(TOKENS).astype(jnp.int32))


def draw_expert_ids(key, part):
    return routing(key)[0]


def draw_slot_index(key, part):
    return routing(key)[1]


def segment_draw(key):
    flag_key = jax.random.fold_in(key, 11)
    groups = TOKENS // SEQ
    pairs = SEQ // 2
    half_pairs = pairs // 2

    def one_group(group_key):
        pick_key, side_key = jax.random.split(group_key)
        picks = jax.random.permutation(pick_key, half_pairs - 1)[:3] + 1
        late_side = jax.random.randint(side_key, (), 0, 2)
        picks = picks + late_side * (pairs - half_pairs)
        return jnp.zeros((pairs,), jnp.int32).at[picks].set(1)
    flags = jax.vmap(one_group)(jax.random.split(flag_key, groups))
    pair_ids = jnp.cumsum(flags, axis=1)
    return jnp.repeat(pair_ids, 2, axis=1).reshape(TOKENS).astype(jnp.int32)


def draw_segment_ids(key, part):
    return segment_draw(key)


def attention_rows(key):
    query_key, rows_key = jax.random.split(jax.random.fold_in(key, 5), 2)
    queries = jnp.clip(jax.random.normal(query_key, (TOKENS, HD)), -6.0, 6.0)
    key_block = jnp.clip(jax.random.normal(rows_key, (TOKENS, HD)), -6.0, 6.0)
    return (queries.astype(jnp.bfloat16), key_block.astype(jnp.bfloat16))


def draw_query_rows(key, part):
    return attention_rows(key)[0]


def draw_key_rows(key, part):
    return attention_rows(key)[1]


def with_spikes(result, rng, source, target, blocks, factor):
    def block_of(axis_at):
        return (jnp.arange(result.shape[axis_at]) // (result.shape[axis_at] // blocks)).reshape((-1,) + (1,) * (result.ndim - 1 - axis_at))

    near = jax.random.permutation(rng, blocks)[block_of(target)]
    other_side = (block_of(target) + blocks // 2) % blocks
    return jnp.where((block_of(source) == near) | (block_of(source) == other_side), factor * result, result)


def block_scale(key, shape, cuts, least, largest):
    level, own = 1.0, jax.random.fold_in(key, 6)
    for dim, shards_of in cuts:
        draws = jnp.exp(jax.random.uniform(jax.random.fold_in(own, dim), (shards_of,), jnp.float32, least / len(cuts), largest / len(cuts)))
        level = level * jnp.repeat(draws, shape[dim] // shards_of).reshape([-1 if axis == dim else 1 for axis in range(len(shape))])
    return level


def scatter_about(key, dims, scale, most, cuts=(), kind=jnp.bfloat16):
    drawn = scale * jax.random.normal(key, dims, jnp.float32)
    if cuts:
        drawn = drawn * block_scale(key, dims, cuts, -0.22, 0.18)
    return jnp.clip(drawn, -most, most).astype(kind)


def heavy_noise(key, shape, deviation, limit, cuts, heavy, kind=jnp.bfloat16):
    values = deviation * jax.random.normal(key, shape, jnp.float32)
    if cuts:
        values = values * block_scale(key, shape, cuts, -0.22, 0.18)
    return jnp.clip(with_spikes(values, jax.random.fold_in(key, 3), *heavy), -limit, limit).astype(kind)


def setup_inputs(seed: int = 0) -> dict:
    splits = jax.random.split(jax.random.key(seed), 21)
    layer_input = draw_layer_input(jax.random.fold_in(splits[20], 71), 0)
    residual = draw_residual(jax.random.fold_in(splits[20], 71), 0)
    out_grad = heavy_noise(splits[2], (TOKENS, D), 1.0, 6.0, ((0, 32),), (0, 1, 32, 2.75))
    gate_prob = jnp.clip(0.2 + 0.8 * jax.random.uniform(splits[3], (TOKENS,), jnp.float32) ** block_scale(splits[3], (TOKENS,), ((0, 32),), -0.2, 0.2), 0.2, 1.0)
    expert_ids = draw_expert_ids(jax.random.fold_in(splits[20], 71), 0)
    slot_index = draw_slot_index(jax.random.fold_in(splits[20], 71), 0)
    segment_ids = draw_segment_ids(jax.random.fold_in(splits[20], 71), 0)
    query_rows = draw_query_rows(jax.random.fold_in(splits[20], 71), 0)
    key_rows = draw_key_rows(jax.random.fold_in(splits[20], 71), 0)
    value_rows = scatter_about(splits[9], (TOKENS, HD), 1.0, 6.0, ((0, 8), (1, 4)))
    attn_heads = scatter_about(splits[10], (TOKENS, HD), 1.0, 6.0, ((0, 8), (1, 4)))
    attn_gain = jnp.clip(1.0 + 0.1 * jax.random.normal(splits[11], (D,), jnp.float32), 0.5, 1.5)
    expert_gain = jnp.clip(1.0 + 0.1 * jax.random.normal(splits[12], (D,), jnp.float32), 0.5, 1.5)
    query_weight = scatter_about(splits[13], (D, HD), D ** -0.5, 0.125, ((1, 4),))
    key_weight = scatter_about(splits[14], (D, HD), D ** -0.5, 0.125, ((1, 4),))
    value_weight = scatter_about(splits[15], (D, HD), D ** -0.5, 0.125, ((1, 4),))
    output_weight = scatter_about(splits[16], (HD, D), HD ** -0.5, 0.1875, ((0, 4),))
    inner_weight = scatter_about(splits[17], (EXPERTS, D, FF), D ** -0.5, 0.125, ((0, 8), (2, 4)))
    outer_weight = scatter_about(splits[18], (EXPERTS, FF, D), FF ** -0.5, 0.109375, ((0, 8), (1, 4)))
    hidden_pre = scatter_about(splits[19], (EXPERTS, N_TENSOR, N_EXPERT, CAP, FF), 1.0, 6.0, ((0, 8), (4, 4)))
    return dict(layer_input=layer_input, residual=residual, out_grad=out_grad, gate_prob=gate_prob, expert_ids=expert_ids, slot_index=slot_index, segment_ids=segment_ids, query_rows=query_rows, key_rows=key_rows, value_rows=value_rows, attn_heads=attn_heads, attn_gain=attn_gain, expert_gain=expert_gain, query_weight=query_weight, key_weight=key_weight, value_weight=value_weight, output_weight=output_weight, inner_weight=inner_weight, outer_weight=outer_weight, hidden_pre=hidden_pre)


EPS = 1e-06

def inv_rms(row_data):
    wide_rows = row_data.astype(jnp.float32)
    return lax.rsqrt(lax.optimization_barrier(jnp.mean(wide_rows * wide_rows, axis=-1, keepdims=True)) + EPS)

def norm_back(grad_rows, row_data, inv_rows, gain_row):
    wide_rows = row_data.astype(jnp.float32)
    scaled = grad_rows * gain_row
    return inv_rows * (scaled - wide_rows * inv_rows * inv_rows * lax.optimization_barrier(jnp.mean(scaled * wide_rows, axis=-1, keepdims=True)))

def block_round_sum(parts):
    return lax.optimization_barrier(jnp.sum(lax.optimization_barrier(parts.astype(jnp.bfloat16)).astype(jnp.float32), axis=0))

def expert_back(packed):
    token_rows, grad_rows, pre_rows, in_weight, back_weight = packed
    row_count = token_rows.shape[0]
    shard_width = in_weight.shape[1] // N_TENSOR
    active = jnp.maximum(pre_rows, 0)
    up_grad = jnp.dot(grad_rows, back_weight.T, preferred_element_type=jnp.float32)
    pre_grad = jnp.where(pre_rows > 0, up_grad, 0.0).astype(jnp.bfloat16)
    gate_parts = lax.optimization_barrier(jnp.sum((active.astype(jnp.float32) * up_grad).reshape(row_count, N_TENSOR, shard_width), axis=2))
    gate_total = block_round_sum(gate_parts.T).astype(jnp.bfloat16)
    input_parts = jnp.einsum('rbf,dbf->brd', pre_grad.astype(jnp.float32).reshape(row_count, N_TENSOR, shard_width), in_weight.astype(jnp.float32).reshape(-1, N_TENSOR, shard_width))
    input_total = block_round_sum(input_parts).astype(jnp.bfloat16)
    inner_sum = jnp.dot(token_rows.T, pre_grad, preferred_element_type=jnp.float32).astype(jnp.bfloat16)
    outer_sum = jnp.dot(active.T, grad_rows, preferred_element_type=jnp.float32).astype(jnp.bfloat16)
    return (inner_sum, outer_sum, input_total, gate_total)

def reference(layer_input, residual, out_grad, gate_prob, expert_ids, slot_index, segment_ids, query_rows, key_rows, value_rows, attn_heads, attn_gain, expert_gain, query_weight, key_weight, value_weight, output_weight, inner_weight, outer_weight, hidden_pre):
    inv_mid = inv_rms(residual)
    normed_mid = (residual.astype(jnp.float32) * inv_mid * expert_gain).astype(jnp.bfloat16)
    scaled_grad = (gate_prob[:, None] * out_grad.astype(jnp.float32)).astype(jnp.bfloat16)
    token_index = jnp.arange(TOKENS, dtype=jnp.int32)
    device = token_index // TOK_DEV
    source_group = device // N_TENSOR
    source_shard = device % N_TENSOR
    kept_mask = slot_index >= 0
    slot_safe = jnp.where(kept_mask, slot_index, CAP).astype(jnp.int32)
    empty_slots = jnp.zeros((EXPERTS, N_TENSOR, N_EXPERT, CAP + 1, D), jnp.bfloat16)
    rows_all = empty_slots.at[expert_ids, source_shard, source_group, slot_safe].set(normed_mid)[:, :, :, :CAP]
    grads_all = empty_slots.at[expert_ids, source_shard, source_group, slot_safe].set(scaled_grad)[:, :, :, :CAP]
    rows_per = N_TENSOR * N_EXPERT * CAP
    inner_grad, outer_grad, input_back, gate_back = lax.map(expert_back, (rows_all.reshape(EXPERTS, rows_per, D), grads_all.reshape(EXPERTS, rows_per, D), hidden_pre.reshape(EXPERTS, rows_per, FF), inner_weight, outer_weight))
    input_back = input_back.reshape(EXPERTS, N_TENSOR, N_EXPERT, CAP, D)
    gate_back = gate_back.reshape(EXPERTS, N_TENSOR, N_EXPERT, CAP)
    slot_read = jnp.where(kept_mask, slot_index, 0).astype(jnp.int32)
    mid_grad = jnp.where(kept_mask[:, None], input_back[expert_ids, source_shard, source_group, slot_read].astype(jnp.float32), 0.0)
    gate_grad = jnp.where(kept_mask, gate_back[expert_ids, source_shard, source_group, slot_read], jnp.zeros((), jnp.bfloat16))
    expert_gain_grad = lax.optimization_barrier(jnp.sum(mid_grad * residual.astype(jnp.float32) * inv_mid, axis=0))
    resid_grad = out_grad.astype(jnp.float32) + norm_back(mid_grad, residual, inv_mid, expert_gain)
    resid_low = resid_grad.astype(jnp.bfloat16)
    inv_in = inv_rms(layer_input)
    normed_in = (layer_input.astype(jnp.float32) * inv_in * attn_gain).astype(jnp.bfloat16)
    score_scale = DH ** (-0.5)
    shard_cols = HD // N_TENSOR

    def by_head(matrix):
        return matrix.reshape(SEQ, HEADS, DH).transpose(1, 0, 2)

    def from_heads(matrix):
        return matrix.transpose(1, 0, 2).reshape(SEQ, HD)

    def partial_sum(grad_cols, weight_cols):
        return jnp.einsum('sbh,dbh->bsd', grad_cols.astype(jnp.float32).reshape(SEQ, N_TENSOR, shard_cols), weight_cols.astype(jnp.float32).reshape(D, N_TENSOR, shard_cols))

    def group_back(inputs):
        grad_seq, normed_seq, queries, key_seq, value_seq, heads_seq, segs = inputs
        head_grad = jnp.dot(grad_seq, output_weight.T, preferred_element_type=jnp.float32).astype(jnp.bfloat16)
        out_part = jnp.dot(heads_seq.T, grad_seq, preferred_element_type=jnp.float32).astype(jnp.bfloat16)
        positions = jnp.arange(SEQ, dtype=jnp.int32)
        allowed = (positions[:, None] >= positions[None, :]) & (segs[:, None] == segs[None, :])

        def head_back(parts):
            query_head, key_head, value_head, heads_head, grad_head = parts
            scores = jnp.dot(query_head, key_head.T, preferred_element_type=jnp.float32) * score_scale
            scores = jnp.where(allowed, scores, -jnp.inf)
            row_top = lax.optimization_barrier(jnp.max(scores, axis=1, keepdims=True))
            weights = jnp.exp(scores - row_top)
            attend = weights / lax.optimization_barrier(jnp.sum(weights, axis=1, keepdims=True))
            row_dot = lax.optimization_barrier(jnp.sum(grad_head.astype(jnp.float32) * heads_head.astype(jnp.float32), axis=1, keepdims=True))
            attend_grad = jnp.dot(grad_head, value_head.T, preferred_element_type=jnp.float32)
            score_grad = (attend * (attend_grad - row_dot) * score_scale).astype(jnp.bfloat16)
            attend_low = attend.astype(jnp.bfloat16)
            query_back = jnp.dot(score_grad, key_head, preferred_element_type=jnp.float32).astype(jnp.bfloat16)
            key_back = jnp.dot(score_grad.T, query_head, preferred_element_type=jnp.float32).astype(jnp.bfloat16)
            value_back = jnp.dot(attend_low.T, grad_head, preferred_element_type=jnp.float32).astype(jnp.bfloat16)
            return (query_back, key_back, value_back)
        query_back, key_back, value_back = lax.map(head_back, (by_head(queries), by_head(key_seq), by_head(value_seq), by_head(heads_seq), by_head(head_grad)))
        query_back = from_heads(query_back)
        key_back = from_heads(key_back)
        value_back = from_heads(value_back)
        parts = partial_sum(query_back, query_weight) + partial_sum(key_back, key_weight) + partial_sum(value_back, value_weight)
        normed_grad = block_round_sum(parts)
        query_part = jnp.dot(normed_seq.T, query_back, preferred_element_type=jnp.float32).astype(jnp.bfloat16)
        key_part = jnp.dot(normed_seq.T, key_back, preferred_element_type=jnp.float32).astype(jnp.bfloat16)
        value_part = jnp.dot(normed_seq.T, value_back, preferred_element_type=jnp.float32).astype(jnp.bfloat16)
        return (normed_grad, query_part, key_part, value_part, out_part)

    def by_group(matrix):
        return matrix.reshape(N_EXPERT, SEQ, matrix.shape[-1])
    normed_grad, query_parts, key_parts, value_parts, out_parts = lax.map(group_back, (by_group(resid_low), by_group(normed_in), by_group(query_rows), by_group(key_rows), by_group(value_rows), by_group(attn_heads), segment_ids.reshape(N_EXPERT, SEQ)))
    normed_grad = normed_grad.reshape(TOKENS, D)

    def group_total(parts):
        return lax.optimization_barrier(jnp.sum(parts.astype(jnp.float32), axis=0)).astype(jnp.bfloat16)
    attn_gain_grad = lax.optimization_barrier(jnp.sum(normed_grad * layer_input.astype(jnp.float32) * inv_in, axis=0))
    input_grad = (resid_grad + norm_back(normed_grad, layer_input, inv_in, attn_gain)).astype(jnp.bfloat16)
    return (input_grad, attn_gain_grad, expert_gain_grad, group_total(query_parts), group_total(key_parts), group_total(value_parts), group_total(out_parts), inner_grad, outer_grad, gate_grad)
```

```python
import jax
import jax.numpy as jnp
from jax import lax
from jax.sharding import PartitionSpec as P

DH = 64


EPS = 1e-06

F32 = jnp.float32
BF16 = jnp.bfloat16

MOST_PERMUTES = 8


def inv_rms(row_data):
    wide_rows = row_data.astype(F32)
    return lax.rsqrt(jnp.mean(wide_rows * wide_rows, axis=-1, keepdims=True) + EPS)


def norm_back(grad_rows, row_data, inv_rows, gain_row):
    wide_rows = row_data.astype(F32)
    scaled = grad_rows * gain_row
    return inv_rows * (
        scaled
        - wide_rows * inv_rows * inv_rows * jnp.mean(scaled * wide_rows, axis=-1, keepdims=True)
    )


def contract_last(left, right):
    return lax.dot_general(left, right, (((1,), (1,)), ((), ())), preferred_element_type=F32)


def contract_first(left, right):
    return lax.dot_general(left, right, (((0,), (0,)), ((), ())), preferred_element_type=F32)


def flip(value, axis, mask):
    count = lax.axis_size(axis)
    return lax.ppermute(value, axis, [(at, at ^ mask) for at in range(count)])


def bits_of(axis):
    return lax.axis_size(axis).bit_length() - 1


def gather_rel(value, axis):
    held = {0: value}
    for bit in reversed(range(bits_of(axis))):
        for rel in list(held):
            held[rel | (1 << bit)] = flip(held[rel], axis, 1 << bit)
    return [held[rel] for rel in range(len(held))]


def pick_rel(blocks, index, count):
    return [lax.dynamic_index_in_dim(blocks, index ^ rel, 0, keepdims=False) for rel in range(count)]


def scatter_sum_rel(parts, axis, order):
    if len(parts) > MOST_PERMUTES:
        whole = jnp.stack(pick_rel(jnp.stack(parts), lax.axis_index(axis), len(parts)))
        return lax.psum_scatter(whole, axis, scatter_dimension=0, tiled=False).astype(F32)
    held = dict(enumerate(parts))
    for step, bit in enumerate(order):
        mask = 1 << bit
        last = step == len(order) - 1
        for rel in [r for r in held if r & mask]:
            got = flip(held.pop(rel), axis, mask)
            total = held[rel ^ mask].astype(F32) + got.astype(F32)
            held[rel ^ mask] = total if last else total.astype(BF16)
    return held[0]


def sum_all(value, axes):
    for axis in axes:
        for bit in range(bits_of(axis)):
            value = value + flip(value, axis, 1 << bit)
    return value


def exchange_rel(parts, axis):
    count = len(parts)
    if count > MOST_PERMUTES:
        whole = jnp.stack(pick_rel(jnp.stack(parts), lax.axis_index(axis), count))
        whole = lax.all_to_all(whole, axis, split_axis=0, concat_axis=0, tiled=True)
        return pick_rel(whole, lax.axis_index(axis), count)
    got = {0: parts[0]}
    for rel in reversed(range(1, count)):
        got[rel] = flip(parts[rel], axis, rel)
    return [got[rel] for rel in range(count)]


def attention_back(query_rows, key_rows, value_rows, attn_heads, head_grad, positions, segment_ids):
    score_scale = DH ** (-0.5)
    query_cols, key_cols, value_cols = ([], [], [])
    allowed = (positions[:, None] >= positions[None, :]) & (
        segment_ids[:, None] == segment_ids[None, :]
    )
    for head_index in range(query_rows.shape[1] // DH):
        cols = slice(head_index * DH, head_index * DH + DH)
        queries, keys, values = query_rows[:, cols], key_rows[:, cols], value_rows[:, cols]
        grads = head_grad[:, cols]
        scores = jnp.where(allowed, contract_last(queries, keys) * score_scale, -jnp.inf)
        row_top = jnp.max(scores, axis=1, keepdims=True)
        weights = jnp.exp(scores - row_top)
        attend = weights / jnp.sum(weights, axis=1, keepdims=True)
        row_dot = jnp.sum(
            grads.astype(F32) * attn_heads[:, cols].astype(F32), axis=1, keepdims=True
        )
        attend_grad = contract_last(grads, values)
        score_grad = (attend * (attend_grad - row_dot) * score_scale).astype(BF16)
        attend_low = attend.astype(BF16)
        query_cols.append(jnp.dot(score_grad, keys, preferred_element_type=F32).astype(BF16))
        key_cols.append(contract_first(score_grad, queries).astype(BF16))
        value_cols.append(contract_first(attend_low, grads).astype(BF16))
    return (
        jnp.concatenate(query_cols, axis=1),
        jnp.concatenate(key_cols, axis=1),
        jnp.concatenate(value_cols, axis=1),
    )


def shards(
    layer_input,
    residual,
    out_grad,
    gate_prob,
    expert_ids,
    slot_index,
    segment_ids,
    query_rows,
    key_rows,
    value_rows,
    attn_heads,
    attn_gain,
    expert_gain,
    query_weight,
    key_weight,
    value_weight,
    output_weight,
    inner_weight,
    outer_weight,
    hidden_pre,
):
    tensor_count = lax.axis_size("tensor")
    expert_count = lax.axis_size("expert")
    tensor_at = lax.axis_index("tensor")
    expert_at = lax.axis_index("expert")
    tok_rows, model_width = layer_input.shape
    slot_count = hidden_pre.shape[3]
    unit_count = hidden_pre.shape[4]
    slot_pad = -(-slot_count // 8) * 8
    group_rows = expert_count * slot_pad

    inv_mid = inv_rms(residual)
    normed_mid = (residual.astype(F32) * inv_mid * expert_gain).astype(BF16)
    scaled_grad = (gate_prob[:, None] * out_grad.astype(F32)).astype(BF16)
    target = jnp.where(slot_index >= 0, (expert_ids ^ expert_at) * slot_pad + slot_index, -1)
    placing = (jnp.arange(group_rows, dtype=jnp.int32)[:, None] == target[None, :]).astype(BF16)
    send_grads = jnp.dot(placing, scaled_grad, preferred_element_type=F32).astype(BF16)
    send_rows = jnp.dot(placing, normed_mid, preferred_element_type=F32).astype(BF16)

    def split(rows):
        return [rows[k * slot_pad : (k + 1) * slot_pad] for k in range(expert_count)]

    got_grads = jnp.concatenate(exchange_rel(split(send_grads), "expert"), axis=0)
    grad_blocks = gather_rel(got_grads, "tensor")
    input_blocks = gather_rel(layer_input, "tensor")
    got_rows = jnp.concatenate(exchange_rel(split(send_rows), "expert"), axis=0)
    row_blocks = gather_rel(got_rows, "tensor")

    pre_blocks = []
    for shard_block in pick_rel(hidden_pre[0], tensor_at, tensor_count):
        block = jnp.stack(pick_rel(shard_block, expert_at, expert_count))
        block = jnp.pad(block, ((0, 0), (0, slot_pad - slot_count), (0, 0)))
        pre_blocks.append(block.reshape(group_rows, unit_count))

    parts, pre_grads = [], []
    for grads, pre in zip(grad_blocks, pre_blocks):
        up_grad = contract_last(grads, outer_weight[0])
        pre_grad = jnp.where(pre > 0, up_grad, 0.0).astype(BF16)
        gate_part = jnp.sum(jnp.maximum(pre, 0).astype(F32) * up_grad, axis=1, keepdims=True)
        slot_part = contract_last(pre_grad, inner_weight[0])
        parts.append(jnp.concatenate([slot_part.astype(BF16), gate_part.astype(BF16)], axis=1))
        pre_grads.append(pre_grad)
    tensor_bits = list(range(bits_of("tensor")))
    expert_bits = list(range(bits_of("expert")))
    slot_sum = scatter_sum_rel(parts, "tensor", tensor_bits).astype(BF16)
    back_flat = jnp.concatenate(exchange_rel(split(slot_sum), "expert"), axis=0)

    flat_rows = jnp.concatenate(row_blocks, axis=0)
    flat_pre_grad = jnp.concatenate(pre_grads, axis=0)
    flat_grads = jnp.concatenate(grad_blocks, axis=0)
    active = jnp.maximum(jnp.concatenate(pre_blocks, axis=0), 0)
    inner_grad = contract_first(flat_rows, flat_pre_grad).astype(BF16)[None]
    outer_grad = contract_first(active, flat_grads).astype(BF16)[None]

    token_back = contract_first(placing, back_flat)
    mid_grad = token_back[:, :model_width]
    gate_grad = token_back[:, model_width].astype(BF16)
    wide_residual = residual.astype(F32)
    gain_mid = jnp.sum(mid_grad * wide_residual * inv_mid, axis=0)
    resid_grad = out_grad.astype(F32) + norm_back(mid_grad, residual, inv_mid, expert_gain)
    resid_low = resid_grad.astype(BF16)

    piece = jnp.concatenate(gather_rel(resid_low, "tensor"), axis=0)

    def seq_rel(rows):
        blocks = rows.reshape((tensor_count, tok_rows) + rows.shape[1:])
        return jnp.concatenate(pick_rel(blocks, tensor_at, tensor_count), axis=0)

    query_rel, key_rel, value_rel, heads_rel, segments, positions = (
        seq_rel(rows)
        for rows in (
            query_rows,
            key_rows,
            value_rows,
            attn_heads,
            segment_ids,
            jnp.arange(tensor_count * tok_rows, dtype=jnp.int32),
        )
    )
    head_grad = contract_last(piece, output_weight).astype(BF16)
    out_sum = contract_first(piece, heads_rel).astype(BF16)
    out_width = model_width // expert_count
    out_parts = pick_rel(out_sum.reshape(expert_count, out_width, -1), expert_at, expert_count)
    out_part = scatter_sum_rel(out_parts, "expert", expert_bits)

    query_back, key_back, value_back = attention_back(
        query_rel, key_rel, value_rel, heads_rel, head_grad, positions, segments
    )
    normed_parts = (
        contract_last(query_back, query_weight)
        + contract_last(key_back, key_weight)
        + contract_last(value_back, value_weight)
    ).astype(BF16)
    normed_grad = scatter_sum_rel(
        [normed_parts[r * tok_rows : (r + 1) * tok_rows] for r in range(tensor_count)],
        "tensor",
        tensor_bits,
    )

    input_seq = jnp.concatenate(input_blocks, axis=0)
    normed_seq = (input_seq.astype(F32) * inv_rms(input_seq) * attn_gain).astype(BF16)
    feature_blocks = jnp.stack(
        [
            lax.dynamic_slice_in_dim(normed_seq, (expert_at ^ k) * out_width, out_width, 1)
            for k in range(expert_count)
        ]
    )
    back_cols = jnp.concatenate([query_back, key_back, value_back], axis=1)
    half_cols = back_cols.shape[1] // 2
    sums = []
    for cols, order in (
        (back_cols[:, :half_cols], expert_bits),
        (back_cols[:, half_cols:], expert_bits[1:] + expert_bits[:1]),
    ):
        shares = lax.dot_general(
            feature_blocks,
            jnp.broadcast_to(cols, (expert_count,) + cols.shape),
            (((1,), (1,)), ((0,), (0,))),
            preferred_element_type=F32,
        ).astype(BF16)
        sums.append(
            scatter_sum_rel([shares[k] for k in range(expert_count)], "expert", order)
        )
    weight_grads = jnp.concatenate(sums, axis=1).astype(BF16)
    query_part, key_part, value_part = jnp.split(weight_grads, 3, axis=1)

    inv_in = inv_rms(layer_input)
    gain_in = jnp.sum(normed_grad * layer_input.astype(F32) * inv_in, axis=0)
    gains = sum_all(jnp.stack([gain_in, gain_mid]), ("tensor", "expert"))
    input_grad = (resid_grad + norm_back(normed_grad, layer_input, inv_in, attn_gain)).astype(BF16)
    return (
        input_grad,
        gains[0],
        gains[1],
        query_part,
        key_part,
        value_part,
        out_part.astype(BF16).T,
        inner_grad,
        outer_grad,
        gate_grad,
    )


def solution(mesh):
    return jax.shard_map(
        shards,
        mesh=mesh,
        in_specs=(
            P(("expert", "tensor"), None),
            P(("expert", "tensor"), None),
            P(("expert", "tensor"), None),
            P(("expert", "tensor")),
            P(("expert", "tensor")),
            P(("expert", "tensor")),
            P("expert"),
            P("expert", "tensor"),
            P("expert", "tensor"),
            P("expert", "tensor"),
            P("expert", "tensor"),
            P(),
            P(),
            P(None, "tensor"),
            P(None, "tensor"),
            P(None, "tensor"),
            P("tensor", None),
            P("expert", None, "tensor"),
            P("expert", "tensor", None),
            P("expert", None, None, None, "tensor"),
        ),
        out_specs=(
            P(("expert", "tensor"), None),
            P(),
            P(),
            P("expert", "tensor"),
            P("expert", "tensor"),
            P("expert", "tensor"),
            P("tensor", "expert"),
            P("expert", None, "tensor"),
            P("expert", "tensor", None),
            P(("expert", "tensor")),
        ),
        check_vma=False,
    )
```

```python
import jax
import jax.numpy as jnp
from jax import lax
from jax.experimental import pallas as pl
from jax.experimental.pallas import tpu as pltpu
from jax.sharding import PartitionSpec as P

DH = 64


EPS = 1e-06

F32 = jnp.float32
BF16 = jnp.bfloat16

MOST_PERMUTES = 8


def inv_rms(row_data):
    wide_rows = row_data.astype(F32)
    return lax.rsqrt(jnp.mean(wide_rows * wide_rows, axis=-1, keepdims=True) + EPS)


def norm_back(grad_rows, row_data, inv_rows, gain_row):
    wide_rows = row_data.astype(F32)
    scaled = grad_rows * gain_row
    return inv_rows * (
        scaled
        - wide_rows * inv_rows * inv_rows * jnp.mean(scaled * wide_rows, axis=-1, keepdims=True)
    )


def contract_last(left, right):
    return lax.dot_general(left, right, (((1,), (1,)), ((), ())), preferred_element_type=F32)


def contract_first(left, right):
    return lax.dot_general(left, right, (((0,), (0,)), ((), ())), preferred_element_type=F32)


def flip(value, axis, mask):
    count = lax.axis_size(axis)
    return lax.ppermute(value, axis, [(at, at ^ mask) for at in range(count)])


def bits_of(axis):
    return lax.axis_size(axis).bit_length() - 1


def gather_rel(value, axis):
    held = {0: value}
    for bit in reversed(range(bits_of(axis))):
        for rel in list(held):
            held[rel | (1 << bit)] = flip(held[rel], axis, 1 << bit)
    return [held[rel] for rel in range(len(held))]


def pick_rel(blocks, index, count):
    return [lax.dynamic_index_in_dim(blocks, index ^ rel, 0, keepdims=False) for rel in range(count)]


def scatter_sum_rel(parts, axis, order):
    if len(parts) > MOST_PERMUTES:
        whole = jnp.stack(pick_rel(jnp.stack(parts), lax.axis_index(axis), len(parts)))
        return lax.psum_scatter(whole, axis, scatter_dimension=0, tiled=False).astype(F32)
    held = dict(enumerate(parts))
    for step, bit in enumerate(order):
        mask = 1 << bit
        last = step == len(order) - 1
        for rel in [r for r in held if r & mask]:
            got = flip(held.pop(rel), axis, mask)
            total = held[rel ^ mask].astype(F32) + got.astype(F32)
            held[rel ^ mask] = total if last else total.astype(BF16)
    return held[0]


def sum_all(value, axes):
    for axis in axes:
        for bit in range(bits_of(axis)):
            value = value + flip(value, axis, 1 << bit)
    return value


def exchange_rel(parts, axis):
    count = len(parts)
    if count > MOST_PERMUTES:
        whole = jnp.stack(pick_rel(jnp.stack(parts), lax.axis_index(axis), count))
        whole = lax.all_to_all(whole, axis, split_axis=0, concat_axis=0, tiled=True)
        return pick_rel(whole, lax.axis_index(axis), count)
    got = {0: parts[0]}
    for rel in reversed(range(1, count)):
        got[rel] = flip(parts[rel], axis, rel)
    return [got[rel] for rel in range(count)]


def halving_order(order):
    places = 1 << len(order)
    last = len(order) - 1
    return [
        sum(((place >> (last - at)) & 1) << bit for at, bit in enumerate(order))
        for place in range(places)
    ]


def halve_sum(shares, axis, order):
    for step, bit in enumerate(order):
        half = shares.shape[0] // 2
        got = flip(shares[half:], axis, 1 << bit)
        shares = shares[:half].astype(F32) + got.astype(F32)
        if step < len(order) - 1:
            shares = shares.astype(BF16)
    return shares


def exchange(blocks, axis):
    return lax.all_to_all(blocks, axis, split_axis=0, concat_axis=0, tiled=True)


def softmax_body(query_ref, key_ref, row_ref, col_ref, out_ref):
    position_q, segment_q = row_ref[0:1, :], row_ref[1:2, :]
    position_k, segment_k = col_ref[:, 0:1], col_ref[:, 1:2]
    allowed = (position_q >= position_k) & (segment_q == segment_k)
    for head in range(query_ref.shape[1] // DH):
        cols = slice(head * DH, head * DH + DH)
        scores = contract_last(key_ref[:, cols], query_ref[:, cols]) * (DH ** (-0.5))
        scores = jnp.where(allowed, scores, -jnp.inf)
        weights = jnp.exp(scores - jnp.max(scores, axis=0, keepdims=True))
        attend = weights / jnp.sum(weights, axis=0, keepdims=True)
        out_ref[head] = attend.astype(BF16)


def softmax_transposed(query_rows, key_rows, positions, segments):
    seq_rows, width = query_rows.shape
    pair = 2 * DH
    by_query = jnp.stack([positions, segments])
    return pl.pallas_call(
        softmax_body,
        grid=(width // pair,),
        in_specs=[
            pl.BlockSpec((seq_rows, pair), lambda at: (0, at)),
            pl.BlockSpec((seq_rows, pair), lambda at: (0, at)),
            pl.BlockSpec((2, seq_rows), lambda at: (0, 0)),
            pl.BlockSpec((seq_rows, 2), lambda at: (0, 0)),
        ],
        out_specs=pl.BlockSpec((2, seq_rows, seq_rows), lambda at: (at, 0, 0)),
        out_shape=jax.ShapeDtypeStruct((width // DH, seq_rows, seq_rows), BF16),
        compiler_params=pltpu.CompilerParams(vmem_limit_bytes=40 << 20),
        cost_estimate=pl.CostEstimate(
            flops=2 * width * seq_rows * seq_rows,
            transcendentals=width // DH * seq_rows * seq_rows,
            bytes_accessed=width // DH * seq_rows * seq_rows * 2,
        ),
    )(query_rows, key_rows, by_query, by_query.T)


def attention_body(attend_ref, query_ref, key_ref, value_ref, heads_ref, grad_ref, out_ref):
    width = query_ref.shape[1]
    products = grad_ref[...].astype(F32) * heads_ref[...].astype(F32)
    products = products.T
    for head in range(width // DH):
        cols = slice(head * DH, head * DH + DH)
        row_dot = jnp.sum(products[cols], axis=0, keepdims=True)
        attend = attend_ref[head]
        grads = grad_ref[:, cols]
        attend_grad = contract_last(value_ref[:, cols], grads)
        score_grad = attend.astype(F32) * (attend_grad - row_dot) * (DH ** (-0.5))
        score_grad = score_grad.astype(BF16)
        for at, back in enumerate(
            (
                contract_first(score_grad, key_ref[:, cols]),
                jnp.dot(score_grad, query_ref[:, cols], preferred_element_type=F32),
                jnp.dot(attend, grads, preferred_element_type=F32),
            )
        ):
            low = at * width + head * DH
            out_ref[:, low : low + DH] = back.astype(BF16)


def attention_back(attend, query_rows, key_rows, value_rows, attn_heads, head_grad, pair_at):
    seq_rows = query_rows.shape[0]
    pair = 2 * DH
    cols = pl.BlockSpec((seq_rows, pair), lambda at: (0, pair_at))
    return pl.pallas_call(
        attention_body,
        grid=(1,),
        in_specs=[
            pl.BlockSpec((2, seq_rows, seq_rows), lambda at: (pair_at, 0, 0)),
            cols,
            cols,
            cols,
            cols,
            cols,
        ],
        out_specs=pl.BlockSpec((seq_rows, 3 * pair), lambda at: (0, 0)),
        out_shape=jax.ShapeDtypeStruct((seq_rows, 3 * pair), BF16),
        compiler_params=pltpu.CompilerParams(vmem_limit_bytes=40 << 20),
        cost_estimate=pl.CostEstimate(
            flops=8 * pair * seq_rows * seq_rows,
            transcendentals=0,
            bytes_accessed=4 * seq_rows * seq_rows + 16 * pair * seq_rows,
        ),
    )(attend, query_rows, key_rows, value_rows, attn_heads, head_grad)


def shards(
    layer_input,
    residual,
    out_grad,
    gate_prob,
    expert_ids,
    slot_index,
    segment_ids,
    query_rows,
    key_rows,
    value_rows,
    attn_heads,
    attn_gain,
    expert_gain,
    query_weight,
    key_weight,
    value_weight,
    output_weight,
    inner_weight,
    outer_weight,
    hidden_pre,
):
    tensor_count = lax.axis_size("tensor")
    expert_count = lax.axis_size("expert")
    tensor_at = lax.axis_index("tensor")
    expert_at = lax.axis_index("expert")
    tok_rows, model_width = layer_input.shape
    slot_count = hidden_pre.shape[3]
    unit_count = hidden_pre.shape[4]
    slot_pad = -(-slot_count // 8) * 8
    group_rows = expert_count * slot_pad

    tensor_bits = list(range(bits_of("tensor")))
    expert_bits = list(range(bits_of("expert")))

    inv_mid = inv_rms(residual)
    normed_mid = (residual.astype(F32) * inv_mid * expert_gain).astype(BF16)
    scaled_grad = (gate_prob[:, None] * out_grad.astype(F32)).astype(BF16)

    def placing_of(experts):
        target = jnp.where(slot_index >= 0, experts * slot_pad + slot_index, -1)
        places = jnp.arange(group_rows, dtype=jnp.int32)
        return (places[:, None] == target[None, :]).astype(BF16)

    def by_expert(rows):
        return rows.reshape(expert_count, slot_pad, -1)

    placing = placing_of(expert_ids)
    send_grads = jnp.dot(placing, scaled_grad, preferred_element_type=F32).astype(BF16)
    send_rows = jnp.dot(placing, normed_mid, preferred_element_type=F32).astype(BF16)
    got_grads = exchange(by_expert(send_grads), "expert").reshape(group_rows, model_width)
    grad_blocks = gather_rel(got_grads, "tensor")
    input_blocks = gather_rel(layer_input, "tensor")
    send_rows, _ = lax.optimization_barrier((send_rows, got_grads))
    got_rows = exchange(by_expert(send_rows), "expert").reshape(group_rows, model_width)

    pre_blocks = []
    for shard_block in pick_rel(hidden_pre[0], tensor_at, tensor_count):
        block = jnp.pad(shard_block, ((0, 0), (0, slot_pad - slot_count), (0, 0)))
        pre_blocks.append(block.reshape(group_rows, unit_count))

    parts, pre_grads = [], []
    for grads, pre in zip(grad_blocks, pre_blocks):
        up_grad = contract_last(grads, outer_weight[0])
        pre_grad = jnp.where(pre > 0, up_grad, 0.0).astype(BF16)
        gate_part = jnp.sum(jnp.maximum(pre, 0).astype(F32) * up_grad, axis=1, keepdims=True)
        slot_part = contract_last(pre_grad, inner_weight[0])
        parts.append(jnp.concatenate([slot_part.astype(BF16), gate_part.astype(BF16)], axis=1))
        pre_grads.append(pre_grad)
    slot_sum = scatter_sum_rel(parts, "tensor", tensor_bits).astype(BF16)
    got_rows, slot_sum = lax.optimization_barrier((got_rows, slot_sum))
    row_blocks = gather_rel(got_rows, "tensor")
    back_parts = pick_rel(by_expert(slot_sum), expert_at, expert_count)
    back_flat = jnp.concatenate(exchange_rel(back_parts, "expert"), axis=0)

    flat_rows = jnp.concatenate(row_blocks, axis=0)
    flat_pre_grad = jnp.concatenate(pre_grads, axis=0)
    flat_grads = jnp.concatenate(grad_blocks, axis=0)
    active = jnp.maximum(jnp.concatenate(pre_blocks, axis=0), 0)
    inner_grad = contract_first(flat_rows, flat_pre_grad).astype(BF16)[None]
    outer_grad = contract_first(active, flat_grads).astype(BF16)[None]

    token_back = contract_first(placing_of(expert_ids ^ expert_at), back_flat)
    mid_grad = token_back[:, :model_width]
    gate_grad = token_back[:, model_width].astype(BF16)
    wide_residual = residual.astype(F32)
    gain_mid = jnp.sum(mid_grad * wide_residual * inv_mid, axis=0)
    resid_grad = out_grad.astype(F32) + norm_back(mid_grad, residual, inv_mid, expert_gain)
    resid_low = resid_grad.astype(BF16)

    seq_order = halving_order(tensor_bits)
    resid_blocks = gather_rel(resid_low, "tensor")
    piece = jnp.concatenate([resid_blocks[rel] for rel in seq_order], axis=0)

    def seq_rel(rows):
        blocks = rows.reshape((tensor_count, tok_rows) + rows.shape[1:])
        picked = pick_rel(blocks, tensor_at, tensor_count)
        return jnp.concatenate([picked[rel] for rel in seq_order], axis=0)

    query_rel, key_rel, value_rel, heads_rel, segments, positions = (
        seq_rel(rows)
        for rows in (
            query_rows,
            key_rows,
            value_rows,
            attn_heads,
            segment_ids,
            jnp.arange(tensor_count * tok_rows, dtype=jnp.int32),
        )
    )
    attend = softmax_transposed(query_rel, key_rel, positions, segments)

    share_rows = model_width // expert_count
    share_pad = -(-share_rows // 8) * 8

    def shares_of(rows, order):
        blocks = [
            jnp.pad(
                lax.dynamic_slice_in_dim(rows, (expert_at ^ rel) * share_rows, share_rows, 0),
                ((0, share_pad - share_rows), (0, 0)),
            )
            for rel in halving_order(order)
        ]
        return jnp.concatenate(blocks, axis=0)

    input_seq = jnp.concatenate([input_blocks[rel] for rel in seq_order], axis=0)
    normed_seq = (input_seq.astype(F32) * inv_rms(input_seq) * attn_gain).astype(BF16)
    normed_cols = normed_seq.T
    pair_orders = [expert_bits, expert_bits[1:] + expert_bits[:1]]
    pair_shares = [shares_of(normed_cols, order) for order in pair_orders]

    head_grad = contract_last(piece, output_weight).astype(BF16)
    out_sum = contract_first(piece, heads_rel).astype(BF16)
    out_part = halve_sum(shares_of(out_sum, expert_bits), "expert", expert_bits)[:share_rows]

    pair = 2 * DH
    weight_sums = []
    normed_parts = 0.0
    for at in range(query_rows.shape[1] // pair):
        back_cols = attention_back(attend, query_rel, key_rel, value_rel, heads_rel, head_grad, at)
        which = at % len(pair_orders)
        shares = jnp.dot(pair_shares[which], back_cols, preferred_element_type=F32).astype(BF16)
        weight_sums.append(halve_sum(shares, "expert", pair_orders[which])[:share_rows])
        for index, weight in enumerate((query_weight, key_weight, value_weight)):
            normed_parts = normed_parts + contract_last(
                back_cols[:, index * pair : (index + 1) * pair],
                weight[:, at * pair : (at + 1) * pair],
            )
    normed_grad = halve_sum(normed_parts.astype(BF16), "tensor", tensor_bits)
    query_part, key_part, value_part = (
        jnp.concatenate(
            [total[:, index * pair : (index + 1) * pair] for total in weight_sums], axis=1
        ).astype(BF16)
        for index in range(3)
    )

    inv_in = inv_rms(layer_input)
    gain_in = jnp.sum(normed_grad * layer_input.astype(F32) * inv_in, axis=0)
    gains = sum_all(jnp.stack([gain_in, gain_mid]), ("tensor", "expert"))
    input_grad = (resid_grad + norm_back(normed_grad, layer_input, inv_in, attn_gain)).astype(BF16)
    return (
        input_grad,
        gains[0],
        gains[1],
        query_part,
        key_part,
        value_part,
        out_part.astype(BF16).T,
        inner_grad,
        outer_grad,
        gate_grad,
    )


def solution(mesh):
    return jax.shard_map(
        shards,
        mesh=mesh,
        in_specs=(
            P(("expert", "tensor"), None),
            P(("expert", "tensor"), None),
            P(("expert", "tensor"), None),
            P(("expert", "tensor")),
            P(("expert", "tensor")),
            P(("expert", "tensor")),
            P("expert"),
            P("expert", "tensor"),
            P("expert", "tensor"),
            P("expert", "tensor"),
            P("expert", "tensor"),
            P(),
            P(),
            P(None, "tensor"),
            P(None, "tensor"),
            P(None, "tensor"),
            P("tensor", None),
            P("expert", None, "tensor"),
            P("expert", "tensor", None),
            P("expert", None, None, None, "tensor"),
        ),
        out_specs=(
            P(("expert", "tensor"), None),
            P(),
            P(),
            P("expert", "tensor"),
            P("expert", "tensor"),
            P("expert", "tensor"),
            P("tensor", "expert"),
            P("expert", None, "tensor"),
            P("expert", "tensor", None),
            P(("expert", "tensor")),
        ),
        check_vma=False,
    )
```

```python
import math

import jax
import jax.numpy as jnp
from jax import lax
from jax.experimental import pallas as pl
from jax.experimental.pallas import tpu as pltpu
from jax.sharding import PartitionSpec as P

DH = 64


EPS = 1e-06

F32 = jnp.float32
BF16 = jnp.bfloat16

MOST_PERMUTES = 8


def inv_rms(row_data):
    wide_rows = row_data.astype(F32)
    return lax.rsqrt(jnp.mean(wide_rows * wide_rows, axis=-1, keepdims=True) + EPS)


def norm_back(grad_rows, row_data, inv_rows, gain_row):
    wide_rows = row_data.astype(F32)
    scaled = grad_rows * gain_row
    return inv_rows * (
        scaled
        - wide_rows * inv_rows * inv_rows * jnp.mean(scaled * wide_rows, axis=-1, keepdims=True)
    )


def contract_last(left, right):
    return lax.dot_general(left, right, (((1,), (1,)), ((), ())), preferred_element_type=F32)


def contract_first(left, right):
    return lax.dot_general(left, right, (((0,), (0,)), ((), ())), preferred_element_type=F32)


def flip(value, axis, mask):
    count = lax.axis_size(axis)
    return lax.ppermute(value, axis, [(at, at ^ mask) for at in range(count)])


def bits_of(axis):
    return lax.axis_size(axis).bit_length() - 1


def gather_rel(value, axis):
    held = {0: value}
    for bit in reversed(range(bits_of(axis))):
        for rel in list(held):
            held[rel | (1 << bit)] = flip(held[rel], axis, 1 << bit)
    return [held[rel] for rel in range(len(held))]


def pick_rel(blocks, index, count):
    return [lax.dynamic_index_in_dim(blocks, index ^ rel, 0, keepdims=False) for rel in range(count)]


def scatter_sum_rel(parts, axis, order):
    held = dict(parts) if isinstance(parts, dict) else dict(enumerate(parts))
    for step, bit in enumerate(order):
        mask = 1 << bit
        last = step == len(order) - 1
        for rel in [r for r in held if r & mask]:
            got = flip(held.pop(rel), axis, mask)
            total = held[rel ^ mask].astype(F32) + got.astype(F32)
            held[rel ^ mask] = total if last else total.astype(BF16)
    return held[0]


def sum_all(value, axes):
    for axis in axes:
        for bit in range(bits_of(axis)):
            value = value + flip(value, axis, 1 << bit)
    return value


def scatter_rel(parts, axis, order):
    held = dict(enumerate(parts))
    for bit in order:
        mask = 1 << bit
        for rel in [r for r in held if r & mask]:
            got = flip(held.pop(rel), axis, mask)
            held[rel ^ mask] = (held[rel ^ mask].astype(F32) + got.astype(F32)).astype(BF16)
    return held


def exchange_rel(parts, axis):
    count = len(parts)
    if count > MOST_PERMUTES:
        whole = jnp.stack(pick_rel(jnp.stack(parts), lax.axis_index(axis), count))
        whole = lax.all_to_all(whole, axis, split_axis=0, concat_axis=0, tiled=True)
        return pick_rel(whole, lax.axis_index(axis), count)
    pad = parts[0].shape[0]
    half = count // 2
    pairs = {0: jnp.concatenate(parts[:2], axis=0)}
    for rel in range(2, count, 2):
        pairs[rel] = flip(jnp.concatenate(parts[rel : rel + 2], axis=0), axis, rel)
    got = {rel: pair[:pad] for rel, pair in pairs.items()}
    for rels in (range(0, half, 2), range(half, count, 2)):
        if len(rels):
            swapped = flip(jnp.concatenate([pairs[rel][pad:] for rel in rels], axis=0), axis, 1)
            for at, rel in enumerate(rels):
                got[rel + 1] = swapped[at * pad : (at + 1) * pad]
    return [got[rel] for rel in range(count)]


def halving_order(order):
    places = 1 << len(order)
    last = len(order) - 1
    return [
        sum(((place >> (last - at)) & 1) << bit for at, bit in enumerate(order))
        for place in range(places)
    ]


def halve_sum(shares, axis, order):
    for step, bit in enumerate(order):
        half = shares.shape[0] // 2
        got = flip(shares[half:], axis, 1 << bit)
        shares = shares[:half].astype(F32) + got.astype(F32)
        if step < len(order) - 1:
            shares = shares.astype(BF16)
    return shares


def exchange(blocks, axis):
    return lax.all_to_all(blocks, axis, split_axis=0, concat_axis=0, tiled=True)


def softmax_body(query_ref, key_ref, row_ref, col_ref, out_ref):
    position_q, segment_q = row_ref[0:1, :], row_ref[1:2, :]
    position_k, segment_k = col_ref[:, 0:1], col_ref[:, 1:2]
    allowed = (position_q >= position_k) & (segment_q == segment_k)
    for head in range(query_ref.shape[1] // DH):
        cols = slice(head * DH, head * DH + DH)
        scores = contract_last(key_ref[:, cols], query_ref[:, cols]) * (DH ** (-0.5))
        scores = jnp.where(allowed, scores, -jnp.inf)
        weights = jnp.exp(scores - jnp.max(scores, axis=0, keepdims=True))
        attend = weights / jnp.sum(weights, axis=0, keepdims=True)
        out_ref[head] = attend.astype(BF16)


def softmax_transposed(query_rows, key_rows, positions, segments):
    seq_rows, width = query_rows.shape
    pair = 2 * DH
    by_query = jnp.stack([positions, segments])
    return pl.pallas_call(
        softmax_body,
        grid=(width // pair,),
        in_specs=[
            pl.BlockSpec((seq_rows, pair), lambda at: (0, at)),
            pl.BlockSpec((seq_rows, pair), lambda at: (0, at)),
            pl.BlockSpec((2, seq_rows), lambda at: (0, 0)),
            pl.BlockSpec((seq_rows, 2), lambda at: (0, 0)),
        ],
        out_specs=pl.BlockSpec((2, seq_rows, seq_rows), lambda at: (at, 0, 0)),
        out_shape=jax.ShapeDtypeStruct((width // DH, seq_rows, seq_rows), BF16),
        compiler_params=pltpu.CompilerParams(vmem_limit_bytes=40 << 20),
        cost_estimate=pl.CostEstimate(
            flops=2 * width * seq_rows * seq_rows,
            transcendentals=width // DH * seq_rows * seq_rows,
            bytes_accessed=width // DH * seq_rows * seq_rows * 2,
        ),
    )(query_rows, key_rows, by_query, by_query.T)


def attention_body(attend_ref, query_ref, key_ref, value_ref, heads_ref, grad_ref, out_ref):
    width = query_ref.shape[1]
    products = grad_ref[...].astype(F32) * heads_ref[...].astype(F32)
    products = products.T
    for head in range(width // DH):
        cols = slice(head * DH, head * DH + DH)
        row_dot = jnp.sum(products[cols], axis=0, keepdims=True)
        attend = attend_ref[head]
        grads = grad_ref[:, cols]
        attend_grad = contract_last(value_ref[:, cols], grads)
        score_grad = attend.astype(F32) * (attend_grad - row_dot) * (DH ** (-0.5))
        score_grad = score_grad.astype(BF16)
        for at, back in enumerate(
            (
                contract_first(score_grad, key_ref[:, cols]),
                jnp.dot(score_grad, query_ref[:, cols], preferred_element_type=F32),
                jnp.dot(attend, grads, preferred_element_type=F32),
            )
        ):
            low = at * width + head * DH
            out_ref[:, low : low + DH] = back.astype(BF16)


def attention_back(attend, query_rows, key_rows, value_rows, attn_heads, head_grad, pair_at):
    seq_rows = query_rows.shape[0]
    pair = 2 * DH
    cols = pl.BlockSpec((seq_rows, pair), lambda at: (0, pair_at))
    return pl.pallas_call(
        attention_body,
        grid=(1,),
        in_specs=[
            pl.BlockSpec((2, seq_rows, seq_rows), lambda at: (pair_at, 0, 0)),
            cols,
            cols,
            cols,
            cols,
            cols,
        ],
        out_specs=pl.BlockSpec((seq_rows, 3 * pair), lambda at: (0, 0)),
        out_shape=jax.ShapeDtypeStruct((seq_rows, 3 * pair), BF16),
        compiler_params=pltpu.CompilerParams(vmem_limit_bytes=40 << 20),
        cost_estimate=pl.CostEstimate(
            flops=8 * pair * seq_rows * seq_rows,
            transcendentals=0,
            bytes_accessed=4 * seq_rows * seq_rows + 16 * pair * seq_rows,
        ),
    )(attend, query_rows, key_rows, value_rows, attn_heads, head_grad)


def expert_body(
    at_ref,
    near_a,
    far_a,
    near_b,
    far_b,
    pre_a,
    pre_b,
    outer_ref,
    inner_ref,
    out_near_a,
    out_far_a,
    out_near_b,
    out_far_b,
    pre_grad_ref,
    active_ref,
    rows_s,
    pre_s,
    total_s,
    gate_s,
):
    step = pl.program_id(0)
    half, width = near_a.shape
    groups, slots = pre_a.shape[1], pre_a.shape[2]
    slot_pad = 2 * half // groups

    @pl.when(step == 0)
    def _():
        for at, ref in enumerate((near_a, far_a, near_b, far_b)):
            rows_s[at * half : (at + 1) * half, :] = ref[...]
        pre_s[...] = jnp.zeros_like(pre_s)

    for which, ref in enumerate((pre_a, pre_b)):
        for rel in range(groups):
            low = (which * groups + rel) * slot_pad
            pre_s[low : low + slots, :] = ref[0, at_ref[0] ^ rel].astype(F32)
    pre = pre_s[...]
    active = jnp.maximum(pre, 0.0)
    up_grad = jnp.dot(rows_s[...], outer_ref[...], preferred_element_type=F32)
    pre_grad = jnp.where(pre > 0, up_grad, 0.0).astype(BF16)
    pre_grad_ref[...] = pre_grad
    active_ref[...] = active.astype(BF16)
    gate = jnp.sum(active * up_grad, axis=1, keepdims=True)
    slot = contract_last(pre_grad, inner_ref[...])

    @pl.when(step == 0)
    def _():
        total_s[...] = slot
        gate_s[...] = gate

    @pl.when(step > 0)
    def _():
        total_s[...] += slot
        gate_s[...] += gate

    @pl.when(step == pl.num_programs(0) - 1)
    def _():
        for at, ref in enumerate((out_near_a, out_far_a, out_near_b, out_far_b)):
            rows = slice(at * half, (at + 1) * half)
            ref[:, :width] = total_s[rows, :].astype(BF16)
            ref[:, width:] = gate_s[rows, :].astype(BF16)


def expert_pair(expert_at, shard_a, shard_b, grads, hidden_pre, outer_weight, inner_weight):
    half, width = grads[0].shape
    groups, slots, units = hidden_pre.shape[1:]
    rows = 4 * half
    block = math.gcd(units, 256)
    held = pl.BlockSpec((half, width), lambda at, where: (0, 0))
    out = pl.BlockSpec((half, width + 1), lambda at, where: (0, 0))
    by_unit = pl.BlockSpec((rows, block), lambda at, where: (0, at))
    return pl.pallas_call(
        expert_body,
        grid_spec=pltpu.PrefetchScalarGridSpec(
            num_scalar_prefetch=1,
            grid=(units // block,),
            in_specs=[
                held,
                held,
                held,
                held,
                pl.BlockSpec((1, groups, slots, block), lambda at, where: (where[1], 0, 0, at)),
                pl.BlockSpec((1, groups, slots, block), lambda at, where: (where[2], 0, 0, at)),
                pl.BlockSpec((width, block), lambda at, where: (0, at)),
                pl.BlockSpec((width, block), lambda at, where: (0, at)),
            ],
            out_specs=[out, out, out, out, by_unit, by_unit],
            scratch_shapes=[
                pltpu.VMEM((rows, width), BF16),
                pltpu.VMEM((rows, block), F32),
                pltpu.VMEM((rows, width), F32),
                pltpu.VMEM((rows, 1), F32),
            ],
        ),
        out_shape=[jax.ShapeDtypeStruct((half, width + 1), BF16)] * 4
        + [jax.ShapeDtypeStruct((rows, units), BF16)] * 2,
        compiler_params=pltpu.CompilerParams(vmem_limit_bytes=44 << 20),
        cost_estimate=pl.CostEstimate(
            flops=4 * rows * width * units,
            transcendentals=0,
            bytes_accessed=4 * width * units + 8 * rows * width + 6 * rows * units,
        ),
    )(
        jnp.stack([expert_at, shard_a, shard_b]).astype(jnp.int32),
        *grads,
        hidden_pre,
        hidden_pre,
        outer_weight,
        inner_weight,
    )


def shards(
    layer_input,
    residual,
    out_grad,
    gate_prob,
    expert_ids,
    slot_index,
    segment_ids,
    query_rows,
    key_rows,
    value_rows,
    attn_heads,
    attn_gain,
    expert_gain,
    query_weight,
    key_weight,
    value_weight,
    output_weight,
    inner_weight,
    outer_weight,
    hidden_pre,
):
    tensor_count = lax.axis_size("tensor")
    expert_count = lax.axis_size("expert")
    tensor_at = lax.axis_index("tensor")
    expert_at = lax.axis_index("expert")
    tok_rows, model_width = layer_input.shape
    slot_count = hidden_pre.shape[3]
    unit_count = hidden_pre.shape[4]
    slot_pad = -(-slot_count // 8) * 8
    group_rows = expert_count * slot_pad

    tensor_bits = list(range(bits_of("tensor")))
    expert_bits = list(range(bits_of("expert")))

    tensor_bits = list(range(bits_of("tensor")))
    expert_bits = list(range(bits_of("expert")))
    barrier = lax.optimization_barrier

    scaled_grad = (gate_prob[:, None] * out_grad.astype(F32)).astype(BF16)

    def placing_of(experts):
        target = jnp.where(slot_index >= 0, experts * slot_pad + slot_index, -1)
        places = jnp.arange(group_rows, dtype=jnp.int32)
        return (places[:, None] == target[None, :]).astype(BF16)

    def split(rows):
        return [rows[low : low + slot_pad] for low in range(0, rows.shape[0], slot_pad)]

    placing = placing_of(expert_ids ^ expert_at)
    send_grads = jnp.dot(placing, scaled_grad, preferred_element_type=F32).astype(BF16)
    got_grads = exchange_rel(split(send_grads), "expert")
    middle = expert_count // 2
    near_grads = jnp.concatenate(got_grads[:middle], axis=0)
    far_grads = jnp.concatenate(got_grads[middle:], axis=0)
    near_blocks = gather_rel(near_grads, "tensor")
    far_blocks = gather_rel(far_grads, "tensor")
    input_blocks = gather_rel(layer_input, "tensor")

    residual_late, _ = barrier((residual, near_grads))
    inv_mid = inv_rms(residual_late)
    normed_mid = (residual_late.astype(F32) * inv_mid * expert_gain).astype(BF16)
    send_rows = jnp.dot(placing_of(expert_ids), normed_mid, preferred_element_type=F32)
    send_rows, _ = barrier((send_rows.astype(BF16), far_grads))
    got_rows = exchange(send_rows.reshape(expert_count, slot_pad, model_width), "expert")

    near_parts, far_parts = [None] * tensor_count, [None] * tensor_count
    pre_grads, actives = [], []
    for rel in range(0, tensor_count, 2):
        near_a, far_a, near_b, far_b, pre_grad, active = expert_pair(
            expert_at,
            tensor_at ^ rel,
            tensor_at ^ (rel + 1),
            (near_blocks[rel], far_blocks[rel], near_blocks[rel + 1], far_blocks[rel + 1]),
            hidden_pre[0],
            outer_weight[0].T,
            inner_weight[0],
        )
        near_parts[rel], near_parts[rel + 1] = near_a, near_b
        far_parts[rel], far_parts[rel + 1] = far_a, far_b
        pre_grads.append(pre_grad)
        actives.append(active)
    far_sum = scatter_sum_rel(far_parts, "tensor", tensor_bits).astype(BF16)
    near_parts = scatter_rel(near_parts, "tensor", tensor_bits[:-1])
    near_parts, far_sum = barrier((near_parts, far_sum))
    near_sum = scatter_sum_rel(near_parts, "tensor", tensor_bits[-1:]).astype(BF16)
    rows_rel = jnp.concatenate(pick_rel(got_rows, expert_at, expert_count), axis=0)
    back_flat = jnp.concatenate(exchange_rel(split(near_sum) + split(far_sum), "expert"), axis=0)

    token_back = contract_first(placing, back_flat)
    mid_grad = token_back[:, :model_width]
    gate_grad = token_back[:, model_width].astype(BF16)
    wide_residual = residual.astype(F32)
    gain_mid = jnp.sum(mid_grad * wide_residual * inv_mid, axis=0)
    resid_grad = out_grad.astype(F32) + norm_back(mid_grad, residual, inv_mid, expert_gain)
    resid_low, rows_rel = barrier((resid_grad.astype(BF16), rows_rel))

    seq_order = halving_order(tensor_bits)
    resid_blocks = gather_rel(resid_low, "tensor")
    piece = jnp.concatenate([resid_blocks[rel] for rel in seq_order], axis=0)

    def seq_rel(rows):
        blocks = rows.reshape((tensor_count, tok_rows) + rows.shape[1:])
        picked = pick_rel(blocks, tensor_at, tensor_count)
        return jnp.concatenate([picked[rel] for rel in seq_order], axis=0)

    late_rows = barrier((query_rows, key_rows, value_rows, attn_heads, segment_ids, near_grads))
    query_rel, key_rel, value_rel, heads_rel, segments, positions = (
        seq_rel(rows)
        for rows in late_rows[:5] + (jnp.arange(tensor_count * tok_rows, dtype=jnp.int32),)
    )
    attend = softmax_transposed(query_rel, key_rel, positions, segments)

    share_rows = model_width // expert_count
    share_pad = -(-share_rows // 8) * 8

    def shares_of(rows, order):
        blocks = [
            jnp.pad(
                lax.dynamic_slice_in_dim(rows, (expert_at ^ rel) * share_rows, share_rows, 0),
                ((0, share_pad - share_rows), (0, 0)),
            )
            for rel in halving_order(order)
        ]
        return jnp.concatenate(blocks, axis=0)

    input_seq = jnp.concatenate([input_blocks[rel] for rel in seq_order], axis=0)
    input_seq, _ = barrier((input_seq, far_parts[-1]))
    unit_seq = input_seq.astype(F32) * inv_rms(input_seq)
    normed_cols = (unit_seq * attn_gain).astype(BF16).T
    pair_orders = [expert_bits, expert_bits[1:] + expert_bits[:1]]
    pair_shares = [shares_of(normed_cols, order) for order in pair_orders]

    piece, pair_shares, unit_seq = barrier((piece, pair_shares, unit_seq))
    head_grad = contract_last(piece, output_weight).astype(BF16)
    pair = 2 * DH
    backs, shares, normed_parts = [], [], 0.0
    for at in range(query_rows.shape[1] // pair):
        back_cols = attention_back(attend, query_rel, key_rel, value_rel, heads_rel, head_grad, at)
        which = at % len(pair_orders)
        shares.append(
            jnp.dot(pair_shares[which], back_cols, preferred_element_type=F32).astype(BF16)
        )
        backs.append(back_cols)
    backs, shares = barrier((backs, shares))
    for at, back_cols in enumerate(backs):
        for index, weight in enumerate((query_weight, key_weight, value_weight)):
            normed_parts = normed_parts + contract_last(
                back_cols[:, index * pair : (index + 1) * pair],
                weight[:, at * pair : (at + 1) * pair],
            )
    gain_in = jnp.sum(normed_parts * unit_seq, axis=0)
    gains = sum_all(jnp.stack([gain_in, gain_mid]), ("tensor",))
    normed_grad = halve_sum(normed_parts.astype(BF16), "tensor", tensor_bits)

    def step_of(part, bit):
        return halve_sum(part, "expert", [bit])

    orders = [pair_orders[at % len(pair_orders)] for at in range(len(shares))]
    sums = [step_of(part, order[0]).astype(BF16) for part, order in zip(shares, orders)]
    flat_grads = jnp.concatenate(
        [block for both in zip(near_blocks, far_blocks) for block in both], axis=0
    )
    sums[0], piece_late, rows_rel, flat_grads, gains = barrier(
        (sums[0], piece, rows_rel, flat_grads, gains)
    )
    row_blocks = gather_rel(rows_rel, "tensor")
    gains = sum_all(gains, ("expert",))
    out_sum = contract_first(piece_late, heads_rel).astype(BF16)
    out_part = step_of(shares_of(out_sum, expert_bits), expert_bits[0]).astype(BF16)
    for step in range(1, len(expert_bits)):
        last = step == len(expert_bits) - 1
        if last:
            sums[0], gains = barrier((sums[0], gains))
            out_part, row_blocks = barrier((out_part, row_blocks))
        sums = [step_of(part, order[step]) for part, order in zip(sums, orders)]
        out_part = step_of(out_part, expert_bits[step])
        if not last:
            sums = [part.astype(BF16) for part in sums]
            out_part = out_part.astype(BF16)
    out_part = out_part[:share_rows]
    weight_sums = [part[:share_rows] for part in sums]
    query_part, key_part, value_part = (
        jnp.concatenate(
            [total[:, index * pair : (index + 1) * pair] for total in weight_sums], axis=1
        ).astype(BF16)
        for index in range(3)
    )

    flat_rows = jnp.concatenate(row_blocks, axis=0)
    inner_grad = contract_first(flat_rows, jnp.concatenate(pre_grads)).astype(BF16)[None]
    outer_grad = contract_first(jnp.concatenate(actives), flat_grads).astype(BF16)[None]

    inv_in = inv_rms(layer_input)
    input_grad = (resid_grad + norm_back(normed_grad, layer_input, inv_in, attn_gain)).astype(BF16)
    return (
        input_grad,
        gains[0],
        gains[1],
        query_part,
        key_part,
        value_part,
        out_part.astype(BF16).T,
        inner_grad,
        outer_grad,
        gate_grad,
    )


def solution(mesh):
    return jax.shard_map(
        shards,
        mesh=mesh,
        in_specs=(
            P(("expert", "tensor"), None),
            P(("expert", "tensor"), None),
            P(("expert", "tensor"), None),
            P(("expert", "tensor")),
            P(("expert", "tensor")),
            P(("expert", "tensor")),
            P("expert"),
            P("expert", "tensor"),
            P("expert", "tensor"),
            P("expert", "tensor"),
            P("expert", "tensor"),
            P(),
            P(),
            P(None, "tensor"),
            P(None, "tensor"),
            P(None, "tensor"),
            P("tensor", None),
            P("expert", None, "tensor"),
            P("expert", "tensor", None),
            P("expert", None, None, None, "tensor"),
        ),
        out_specs=(
            P(("expert", "tensor"), None),
            P(),
            P(),
            P("expert", "tensor"),
            P("expert", "tensor"),
            P("expert", "tensor"),
            P("tensor", "expert"),
            P("expert", None, "tensor"),
            P("expert", "tensor", None),
            P(("expert", "tensor")),
        ),
        check_vma=False,
    )
```

```python
import jax
import jax.numpy as jnp
from jax import lax
from jax.experimental import pallas as pl
from jax.experimental.pallas import tpu as pltpu
from jax.sharding import PartitionSpec as P

DH = 64


EPS = 1e-06

F32 = jnp.float32
BF16 = jnp.bfloat16

MOST_PERMUTES = 8


def inv_rms(row_data):
    wide_rows = row_data.astype(F32)
    return lax.rsqrt(jnp.mean(wide_rows * wide_rows, axis=-1, keepdims=True) + EPS)


def norm_back(grad_rows, row_data, inv_rows, gain_row):
    wide_rows = row_data.astype(F32)
    scaled = grad_rows * gain_row
    return inv_rows * (
        scaled
        - wide_rows * inv_rows * inv_rows * jnp.mean(scaled * wide_rows, axis=-1, keepdims=True)
    )


def contract_last(left, right):
    return lax.dot_general(left, right, (((1,), (1,)), ((), ())), preferred_element_type=F32)


def contract_first(left, right):
    return lax.dot_general(left, right, (((0,), (0,)), ((), ())), preferred_element_type=F32)


def flip(value, axis, mask):
    count = lax.axis_size(axis)
    return lax.ppermute(value, axis, [(at, at ^ mask) for at in range(count)])


def bits_of(axis):
    return lax.axis_size(axis).bit_length() - 1


def gather_rel(value, axis):
    held = {0: value}
    for bit in reversed(range(bits_of(axis))):
        for rel in list(held):
            held[rel | (1 << bit)] = flip(held[rel], axis, 1 << bit)
    return [held[rel] for rel in range(len(held))]


def pick_rel(blocks, index, count):
    return [lax.dynamic_index_in_dim(blocks, index ^ rel, 0, keepdims=False) for rel in range(count)]


def scatter_sum_rel(parts, axis, order):
    if len(parts) > MOST_PERMUTES:
        whole = jnp.stack(pick_rel(jnp.stack(parts), lax.axis_index(axis), len(parts)))
        return lax.psum_scatter(whole, axis, scatter_dimension=0, tiled=False).astype(F32)
    held = dict(enumerate(parts))
    for step, bit in enumerate(order):
        mask = 1 << bit
        last = step == len(order) - 1
        for rel in [r for r in held if r & mask]:
            got = flip(held.pop(rel), axis, mask)
            total = held[rel ^ mask].astype(F32) + got.astype(F32)
            held[rel ^ mask] = total if last else total.astype(BF16)
    return held[0]


def exchange_rel(parts, axis):
    count = len(parts)
    if count > MOST_PERMUTES:
        whole = jnp.stack(pick_rel(jnp.stack(parts), lax.axis_index(axis), count))
        whole = lax.all_to_all(whole, axis, split_axis=0, concat_axis=0, tiled=True)
        return pick_rel(whole, lax.axis_index(axis), count)
    got = {0: parts[0]}
    for rel in reversed(range(1, count)):
        got[rel] = flip(parts[rel], axis, rel)
    return [got[rel] for rel in range(count)]


def halving_order(order):
    places = 1 << len(order)
    last = len(order) - 1
    return [
        sum(((place >> (last - at)) & 1) << bit for at, bit in enumerate(order))
        for place in range(places)
    ]


def split_float(value):
    high = lax.reduce_precision(value, 8, 7)
    return jnp.concatenate([high.astype(BF16), (value - high).astype(BF16)], axis=0)


def halve_with(shares, extra, axis, bit):
    half = shares.shape[0] // 2
    rows = extra.shape[0]
    got = flip(jnp.concatenate([shares[half:], split_float(extra)], axis=0), axis, 1 << bit)
    high, low = got[half : half + rows].astype(F32), got[half + rows :].astype(F32)
    return shares[:half].astype(F32) + got[:half].astype(F32), extra + (high + low)


def halve_sum(shares, axis, order):
    for step, bit in enumerate(order):
        half = shares.shape[0] // 2
        got = flip(shares[half:], axis, 1 << bit)
        shares = shares[:half].astype(F32) + got.astype(F32)
        if step < len(order) - 1:
            shares = shares.astype(BF16)
    return shares


def exchange(blocks, axis):
    return lax.all_to_all(blocks, axis, split_axis=0, concat_axis=0, tiled=True)


def softmax_body(query_ref, key_ref, row_ref, col_ref, out_ref):
    position_q, segment_q = row_ref[0:1, :], row_ref[1:2, :]
    position_k, segment_k = col_ref[:, 0:1], col_ref[:, 1:2]
    allowed = (position_q >= position_k) & (segment_q == segment_k)
    for head in range(query_ref.shape[1] // DH):
        cols = slice(head * DH, head * DH + DH)
        scores = contract_last(key_ref[:, cols], query_ref[:, cols]) * (DH ** (-0.5))
        scores = jnp.where(allowed, scores, -jnp.inf)
        weights = jnp.exp(scores - jnp.max(scores, axis=0, keepdims=True))
        attend = weights / jnp.sum(weights, axis=0, keepdims=True)
        out_ref[head] = attend.astype(BF16)


def softmax_transposed(query_rows, key_rows, positions, segments):
    seq_rows, width = query_rows.shape
    pair = 2 * DH
    by_query = jnp.stack([positions, segments])
    return pl.pallas_call(
        softmax_body,
        grid=(width // pair,),
        in_specs=[
            pl.BlockSpec((seq_rows, pair), lambda at: (0, at)),
            pl.BlockSpec((seq_rows, pair), lambda at: (0, at)),
            pl.BlockSpec((2, seq_rows), lambda at: (0, 0)),
            pl.BlockSpec((seq_rows, 2), lambda at: (0, 0)),
        ],
        out_specs=pl.BlockSpec((2, seq_rows, seq_rows), lambda at: (at, 0, 0)),
        out_shape=jax.ShapeDtypeStruct((width // DH, seq_rows, seq_rows), BF16),
        compiler_params=pltpu.CompilerParams(vmem_limit_bytes=40 << 20),
        cost_estimate=pl.CostEstimate(
            flops=2 * width * seq_rows * seq_rows,
            transcendentals=width // DH * seq_rows * seq_rows,
            bytes_accessed=width // DH * seq_rows * seq_rows * 2,
        ),
    )(query_rows, key_rows, by_query, by_query.T)


def attention_body(attend_ref, query_ref, key_ref, value_ref, heads_ref, grad_ref, out_ref):
    width = query_ref.shape[1]
    products = grad_ref[...].astype(F32) * heads_ref[...].astype(F32)
    products = products.T
    for head in range(width // DH):
        cols = slice(head * DH, head * DH + DH)
        row_dot = jnp.sum(products[cols], axis=0, keepdims=True)
        attend = attend_ref[head]
        grads = grad_ref[:, cols]
        attend_grad = contract_last(value_ref[:, cols], grads)
        score_grad = attend.astype(F32) * (attend_grad - row_dot) * (DH ** (-0.5))
        score_grad = score_grad.astype(BF16)
        for at, back in enumerate(
            (
                contract_first(score_grad, key_ref[:, cols]),
                jnp.dot(score_grad, query_ref[:, cols], preferred_element_type=F32),
                jnp.dot(attend, grads, preferred_element_type=F32),
            )
        ):
            low = at * width + head * DH
            out_ref[:, low : low + DH] = back.astype(BF16)


def attention_back(attend, query_rows, key_rows, value_rows, attn_heads, head_grad, pair_at):
    seq_rows = query_rows.shape[0]
    pair = 2 * DH
    cols = pl.BlockSpec((seq_rows, pair), lambda at: (0, pair_at))
    return pl.pallas_call(
        attention_body,
        grid=(1,),
        in_specs=[
            pl.BlockSpec((2, seq_rows, seq_rows), lambda at: (pair_at, 0, 0)),
            cols,
            cols,
            cols,
            cols,
            cols,
        ],
        out_specs=pl.BlockSpec((seq_rows, 3 * pair), lambda at: (0, 0)),
        out_shape=jax.ShapeDtypeStruct((seq_rows, 3 * pair), BF16),
        compiler_params=pltpu.CompilerParams(vmem_limit_bytes=40 << 20),
        cost_estimate=pl.CostEstimate(
            flops=8 * pair * seq_rows * seq_rows,
            transcendentals=0,
            bytes_accessed=4 * seq_rows * seq_rows + 16 * pair * seq_rows,
        ),
    )(attend, query_rows, key_rows, value_rows, attn_heads, head_grad)


def shards(
    layer_input,
    residual,
    out_grad,
    gate_prob,
    expert_ids,
    slot_index,
    segment_ids,
    query_rows,
    key_rows,
    value_rows,
    attn_heads,
    attn_gain,
    expert_gain,
    query_weight,
    key_weight,
    value_weight,
    output_weight,
    inner_weight,
    outer_weight,
    hidden_pre,
):
    tensor_count = lax.axis_size("tensor")
    expert_count = lax.axis_size("expert")
    tensor_at = lax.axis_index("tensor")
    expert_at = lax.axis_index("expert")
    tok_rows, model_width = layer_input.shape
    slot_count = hidden_pre.shape[3]
    unit_count = hidden_pre.shape[4]
    slot_pad = -(-slot_count // 8) * 8
    group_rows = expert_count * slot_pad

    tensor_bits = list(range(bits_of("tensor")))
    expert_bits = list(range(bits_of("expert")))

    inv_mid = inv_rms(residual)
    normed_mid = (residual.astype(F32) * inv_mid * expert_gain).astype(BF16)
    scaled_grad = (gate_prob[:, None] * out_grad.astype(F32)).astype(BF16)

    def placing_of(experts):
        target = jnp.where(slot_index >= 0, experts * slot_pad + slot_index, -1)
        places = jnp.arange(group_rows, dtype=jnp.int32)
        return (places[:, None] == target[None, :]).astype(BF16)

    def by_expert(rows):
        return rows.reshape(expert_count, slot_pad, -1)

    placing = placing_of(expert_ids)
    send_grads = jnp.dot(placing, scaled_grad, preferred_element_type=F32).astype(BF16)
    send_rows = jnp.dot(placing, normed_mid, preferred_element_type=F32).astype(BF16)
    got_grads = exchange(by_expert(send_grads), "expert").reshape(group_rows, model_width)
    grad_blocks = gather_rel(got_grads, "tensor")
    input_blocks = gather_rel(layer_input, "tensor")
    send_rows, _ = lax.optimization_barrier((send_rows, got_grads))
    got_rows = exchange(by_expert(send_rows), "expert").reshape(group_rows, model_width)

    pre_blocks = []
    for shard_block in pick_rel(hidden_pre[0], tensor_at, tensor_count):
        block = jnp.pad(shard_block, ((0, 0), (0, slot_pad - slot_count), (0, 0)))
        pre_blocks.append(block.reshape(group_rows, unit_count))

    parts, pre_grads = [], []
    for grads, pre in zip(grad_blocks, pre_blocks):
        up_grad = contract_last(grads, outer_weight[0])
        pre_grad = jnp.where(pre > 0, up_grad, 0.0).astype(BF16)
        gate_part = jnp.sum(jnp.maximum(pre, 0).astype(F32) * up_grad, axis=1, keepdims=True)
        slot_part = contract_last(pre_grad, inner_weight[0])
        parts.append(jnp.concatenate([slot_part.astype(BF16), gate_part.astype(BF16)], axis=1))
        pre_grads.append(pre_grad)
    slot_sum = scatter_sum_rel(parts, "tensor", tensor_bits).astype(BF16)
    back_parts = pick_rel(by_expert(slot_sum), expert_at, expert_count)
    back_flat = jnp.concatenate(exchange_rel(back_parts, "expert"), axis=0)

    token_back = contract_first(placing_of(expert_ids ^ expert_at), back_flat)
    mid_grad = token_back[:, :model_width]
    gate_grad = token_back[:, model_width].astype(BF16)
    wide_residual = residual.astype(F32)
    gain_mid = jnp.sum(mid_grad * wide_residual * inv_mid, axis=0)
    resid_grad = out_grad.astype(F32) + norm_back(mid_grad, residual, inv_mid, expert_gain)
    resid_low = resid_grad.astype(BF16)

    seq_order = halving_order(tensor_bits)
    resid_blocks = gather_rel(resid_low, "tensor")
    piece = jnp.concatenate([resid_blocks[rel] for rel in seq_order], axis=0)

    def seq_rel(rows):
        blocks = rows.reshape((tensor_count, tok_rows) + rows.shape[1:])
        picked = pick_rel(blocks, tensor_at, tensor_count)
        return jnp.concatenate([picked[rel] for rel in seq_order], axis=0)

    query_rel, key_rel, value_rel, heads_rel, segments, positions = (
        seq_rel(rows)
        for rows in (
            query_rows,
            key_rows,
            value_rows,
            attn_heads,
            segment_ids,
            jnp.arange(tensor_count * tok_rows, dtype=jnp.int32),
        )
    )
    attend = softmax_transposed(query_rel, key_rel, positions, segments)

    share_rows = model_width // expert_count
    share_pad = -(-share_rows // 8) * 8

    def shares_of(rows, order):
        blocks = [
            jnp.pad(
                lax.dynamic_slice_in_dim(rows, (expert_at ^ rel) * share_rows, share_rows, 0),
                ((0, share_pad - share_rows), (0, 0)),
            )
            for rel in halving_order(order)
        ]
        return jnp.concatenate(blocks, axis=0)

    barrier = lax.optimization_barrier
    input_seq = jnp.concatenate([input_blocks[rel] for rel in seq_order], axis=0)
    input_seq, _ = barrier((input_seq, parts[-1]))
    unit_seq = input_seq.astype(F32) * inv_rms(input_seq)
    normed_cols = (unit_seq * attn_gain).astype(BF16).T
    pair_orders = [expert_bits, expert_bits[1:] + expert_bits[:1]]
    pair_shares = [shares_of(normed_cols, order) for order in pair_orders]
    piece, pair_shares = barrier((piece, pair_shares))

    head_grad = contract_last(piece, output_weight).astype(BF16)
    pair = 2 * DH
    backs, shares, normed_parts = [], [], 0.0
    for at in range(query_rows.shape[1] // pair):
        back_cols = attention_back(attend, query_rel, key_rel, value_rel, heads_rel, head_grad, at)
        which = at % len(pair_orders)
        shares.append(
            jnp.dot(pair_shares[which], back_cols, preferred_element_type=F32).astype(BF16)
        )
        backs.append(back_cols)
    backs, shares = barrier((backs, shares))
    orders = [pair_orders[at % len(pair_orders)] for at in range(len(shares))]
    sums = [halve_sum(part, "expert", order[:1]).astype(BF16) for part, order in zip(shares, orders)]
    for at, back_cols in enumerate(backs):
        for index, weight in enumerate((query_weight, key_weight, value_weight)):
            normed_parts = normed_parts + contract_last(
                back_cols[:, index * pair : (index + 1) * pair],
                weight[:, at * pair : (at + 1) * pair],
            )

    gains = jnp.stack([jnp.sum(normed_parts * unit_seq, axis=0), gain_mid])
    for bit in tensor_bits:
        gains = gains + flip(gains, "tensor", 1 << bit)
    normed_grad = halve_sum(normed_parts.astype(BF16), "tensor", tensor_bits)
    out_width = query_rows.shape[1]
    gain_size = 2 * model_width
    gain_rows = -(-gain_size // (8 * out_width)) * 8
    gains = jnp.pad(gains.reshape(gain_size), (0, gain_rows * out_width - gain_size))
    gains = gains.reshape(gain_rows, out_width)

    flat_grads = jnp.concatenate(grad_blocks, axis=0)
    sums[0], piece_late, got_rows, flat_grads = barrier((sums[0], piece, got_rows, flat_grads))
    row_blocks = gather_rel(got_rows, "tensor")
    out_sum = contract_first(piece_late, heads_rel).astype(BF16)
    out_part = shares_of(out_sum, expert_bits)
    out_part, gains = halve_with(out_part.astype(BF16), gains, "expert", expert_bits[0])
    for step in range(1, len(expert_bits)):
        if step == len(expert_bits) - 1:
            sums[-1], row_blocks = barrier((sums[-1], row_blocks))
        sums = [
            halve_sum(part.astype(BF16), "expert", [order[step]])
            for part, order in zip(sums, orders)
        ]
        if step == 1:
            out_part, sums[0] = barrier((out_part, sums[0]))
        out_part, gains = halve_with(out_part.astype(BF16), gains, "expert", expert_bits[step])
    out_part = out_part[:share_rows]
    weight_sums = [part[:share_rows] for part in sums]
    gains = gains.reshape(gain_rows * out_width)[:gain_size].reshape(2, model_width)
    query_part, key_part, value_part = (
        jnp.concatenate(
            [total[:, index * pair : (index + 1) * pair] for total in weight_sums], axis=1
        ).astype(BF16)
        for index in range(3)
    )

    flat_rows = jnp.concatenate(row_blocks, axis=0)
    active = jnp.maximum(jnp.concatenate(pre_blocks, axis=0), 0)
    inner_grad = contract_first(flat_rows, jnp.concatenate(pre_grads, axis=0)).astype(BF16)[None]
    outer_grad = contract_first(active, flat_grads).astype(BF16)[None]

    inv_in = inv_rms(layer_input)
    input_grad = (resid_grad + norm_back(normed_grad, layer_input, inv_in, attn_gain)).astype(BF16)
    return (
        input_grad,
        gains[0],
        gains[1],
        query_part,
        key_part,
        value_part,
        out_part.astype(BF16).T,
        inner_grad,
        outer_grad,
        gate_grad,
    )


def solution(mesh):
    return jax.shard_map(
        shards,
        mesh=mesh,
        in_specs=(
            P(("expert", "tensor"), None),
            P(("expert", "tensor"), None),
            P(("expert", "tensor"), None),
            P(("expert", "tensor")),
            P(("expert", "tensor")),
            P(("expert", "tensor")),
            P("expert"),
            P("expert", "tensor"),
            P("expert", "tensor"),
            P("expert", "tensor"),
            P("expert", "tensor"),
            P(),
            P(),
            P(None, "tensor"),
            P(None, "tensor"),
            P(None, "tensor"),
            P("tensor", None),
            P("expert", None, "tensor"),
            P("expert", "tensor", None),
            P("expert", None, None, None, "tensor"),
        ),
        out_specs=(
            P(("expert", "tensor"), None),
            P(),
            P(),
            P("expert", "tensor"),
            P("expert", "tensor"),
            P("expert", "tensor"),
            P("tensor", "expert"),
            P("expert", None, "tensor"),
            P("expert", "tensor", None),
            P(("expert", "tensor")),
        ),
        check_vma=False,
    )
```

```python
import jax
import jax.numpy as jnp
from jax import lax
from jax.experimental import pallas as pl
from jax.experimental.pallas import tpu as pltpu
from jax.sharding import PartitionSpec as P

DH = 64


EPS = 1e-06

F32 = jnp.float32
BF16 = jnp.bfloat16

MOST_PERMUTES = 8


def inv_rms(row_data):
    wide_rows = row_data.astype(F32)
    return lax.rsqrt(jnp.mean(wide_rows * wide_rows, axis=-1, keepdims=True) + EPS)


def norm_back(grad_rows, row_data, inv_rows, gain_row):
    wide_rows = row_data.astype(F32)
    scaled = grad_rows * gain_row
    return inv_rows * (
        scaled
        - wide_rows * inv_rows * inv_rows * jnp.mean(scaled * wide_rows, axis=-1, keepdims=True)
    )


def contract_last(left, right):
    return lax.dot_general(left, right, (((1,), (1,)), ((), ())), preferred_element_type=F32)


def contract_first(left, right):
    return lax.dot_general(left, right, (((0,), (0,)), ((), ())), preferred_element_type=F32)


def flip(value, axis, mask):
    count = lax.axis_size(axis)
    return lax.ppermute(value, axis, [(at, at ^ mask) for at in range(count)])


def bits_of(axis):
    return lax.axis_size(axis).bit_length() - 1


def gather_rel(value, axis):
    held = {0: value}
    for bit in reversed(range(bits_of(axis))):
        for rel in list(held):
            held[rel | (1 << bit)] = flip(held[rel], axis, 1 << bit)
    return [held[rel] for rel in range(len(held))]


def pick_rel(blocks, index, count):
    return [lax.dynamic_index_in_dim(blocks, index ^ rel, 0, keepdims=False) for rel in range(count)]


def scatter_sum_rel(parts, axis, order):
    if len(parts) > MOST_PERMUTES:
        whole = jnp.stack(pick_rel(jnp.stack(parts), lax.axis_index(axis), len(parts)))
        return lax.psum_scatter(whole, axis, scatter_dimension=0, tiled=False).astype(F32)
    held = dict(enumerate(parts))
    for step, bit in enumerate(order):
        mask = 1 << bit
        last = step == len(order) - 1
        for rel in [r for r in held if r & mask]:
            got = flip(held.pop(rel), axis, mask)
            total = held[rel ^ mask].astype(F32) + got.astype(F32)
            held[rel ^ mask] = total if last else total.astype(BF16)
    return held[0]


def exchange_rel(parts, axis):
    count = len(parts)
    if count > MOST_PERMUTES:
        whole = jnp.stack(pick_rel(jnp.stack(parts), lax.axis_index(axis), count))
        whole = lax.all_to_all(whole, axis, split_axis=0, concat_axis=0, tiled=True)
        return pick_rel(whole, lax.axis_index(axis), count)
    got = {0: parts[0]}
    for rel in reversed(range(1, count)):
        got[rel] = flip(parts[rel], axis, rel)
    return [got[rel] for rel in range(count)]


def halving_order(order):
    places = 1 << len(order)
    last = len(order) - 1
    return [
        sum(((place >> (last - at)) & 1) << bit for at, bit in enumerate(order))
        for place in range(places)
    ]


def split_float(value):
    high = lax.reduce_precision(value, 8, 7)
    return jnp.concatenate([high.astype(BF16), (value - high).astype(BF16)], axis=0)


def halve_with(shares, extra, axis, bit):
    half = shares.shape[0] // 2
    rows = extra.shape[0]
    got = flip(jnp.concatenate([shares[half:], split_float(extra)], axis=0), axis, 1 << bit)
    high, low = got[half : half + rows].astype(F32), got[half + rows :].astype(F32)
    return shares[:half].astype(F32) + got[:half].astype(F32), extra + (high + low)


def halve_sum(shares, axis, order):
    for step, bit in enumerate(order):
        half = shares.shape[0] // 2
        got = flip(shares[half:], axis, 1 << bit)
        shares = shares[:half].astype(F32) + got.astype(F32)
        if step < len(order) - 1:
            shares = shares.astype(BF16)
    return shares


def exchange(blocks, axis):
    return lax.all_to_all(blocks, axis, split_axis=0, concat_axis=0, tiled=True)


def softmax_body(query_ref, key_ref, row_ref, col_ref, out_ref):
    position_q, segment_q = row_ref[0:1, :], row_ref[1:2, :]
    position_k, segment_k = col_ref[:, 0:1], col_ref[:, 1:2]
    allowed = (position_q >= position_k) & (segment_q == segment_k)
    for head in range(query_ref.shape[1] // DH):
        cols = slice(head * DH, head * DH + DH)
        scores = contract_last(key_ref[:, cols], query_ref[:, cols]) * (DH ** (-0.5))
        scores = jnp.where(allowed, scores, -jnp.inf)
        weights = jnp.exp(scores - jnp.max(scores, axis=0, keepdims=True))
        attend = weights / jnp.sum(weights, axis=0, keepdims=True)
        out_ref[head] = attend.astype(BF16)


def softmax_transposed(query_rows, key_rows, positions, segments):
    seq_rows, width = query_rows.shape
    pair = 2 * DH
    by_query = jnp.stack([positions, segments])
    return pl.pallas_call(
        softmax_body,
        grid=(width // pair,),
        in_specs=[
            pl.BlockSpec((seq_rows, pair), lambda at: (0, at)),
            pl.BlockSpec((seq_rows, pair), lambda at: (0, at)),
            pl.BlockSpec((2, seq_rows), lambda at: (0, 0)),
            pl.BlockSpec((seq_rows, 2), lambda at: (0, 0)),
        ],
        out_specs=pl.BlockSpec((2, seq_rows, seq_rows), lambda at: (at, 0, 0)),
        out_shape=jax.ShapeDtypeStruct((width // DH, seq_rows, seq_rows), BF16),
        compiler_params=pltpu.CompilerParams(vmem_limit_bytes=40 << 20),
        cost_estimate=pl.CostEstimate(
            flops=2 * width * seq_rows * seq_rows,
            transcendentals=width // DH * seq_rows * seq_rows,
            bytes_accessed=width // DH * seq_rows * seq_rows * 2,
        ),
    )(query_rows, key_rows, by_query, by_query.T)


def attention_body(attend_ref, query_ref, key_ref, value_ref, heads_ref, grad_ref, out_ref):
    width = query_ref.shape[1]
    products = grad_ref[...].astype(F32) * heads_ref[...].astype(F32)
    products = products.T
    for head in range(width // DH):
        cols = slice(head * DH, head * DH + DH)
        row_dot = jnp.sum(products[cols], axis=0, keepdims=True)
        attend = attend_ref[head]
        grads = grad_ref[:, cols]
        attend_grad = contract_last(value_ref[:, cols], grads)
        score_grad = attend.astype(F32) * (attend_grad - row_dot) * (DH ** (-0.5))
        score_grad = score_grad.astype(BF16)
        for at, back in enumerate(
            (
                contract_first(score_grad, key_ref[:, cols]),
                jnp.dot(score_grad, query_ref[:, cols], preferred_element_type=F32),
                jnp.dot(attend, grads, preferred_element_type=F32),
            )
        ):
            low = at * width + head * DH
            out_ref[:, low : low + DH] = back.astype(BF16)


def attention_back(attend, query_rows, key_rows, value_rows, attn_heads, head_grad, pair_at):
    seq_rows = query_rows.shape[0]
    pair = 2 * DH
    cols = pl.BlockSpec((seq_rows, pair), lambda at: (0, pair_at))
    return pl.pallas_call(
        attention_body,
        grid=(1,),
        in_specs=[
            pl.BlockSpec((2, seq_rows, seq_rows), lambda at: (pair_at, 0, 0)),
            cols,
            cols,
            cols,
            cols,
            cols,
        ],
        out_specs=pl.BlockSpec((seq_rows, 3 * pair), lambda at: (0, 0)),
        out_shape=jax.ShapeDtypeStruct((seq_rows, 3 * pair), BF16),
        compiler_params=pltpu.CompilerParams(vmem_limit_bytes=40 << 20),
        cost_estimate=pl.CostEstimate(
            flops=8 * pair * seq_rows * seq_rows,
            transcendentals=0,
            bytes_accessed=4 * seq_rows * seq_rows + 16 * pair * seq_rows,
        ),
    )(attend, query_rows, key_rows, value_rows, attn_heads, head_grad)


def shards(
    layer_input,
    residual,
    out_grad,
    gate_prob,
    expert_ids,
    slot_index,
    segment_ids,
    query_rows,
    key_rows,
    value_rows,
    attn_heads,
    attn_gain,
    expert_gain,
    query_weight,
    key_weight,
    value_weight,
    output_weight,
    inner_weight,
    outer_weight,
    hidden_pre,
):
    tensor_count = lax.axis_size("tensor")
    expert_count = lax.axis_size("expert")
    tensor_at = lax.axis_index("tensor")
    expert_at = lax.axis_index("expert")
    tok_rows, model_width = layer_input.shape
    slot_count = hidden_pre.shape[3]
    unit_count = hidden_pre.shape[4]
    slot_pad = -(-slot_count // 8) * 8
    group_rows = expert_count * slot_pad

    tensor_bits = list(range(bits_of("tensor")))
    expert_bits = list(range(bits_of("expert")))

    inv_mid = inv_rms(residual)
    normed_mid = (residual.astype(F32) * inv_mid * expert_gain).astype(BF16)
    scaled_grad = (gate_prob[:, None] * out_grad.astype(F32)).astype(BF16)

    def placing_of(experts):
        target = jnp.where(slot_index >= 0, experts * slot_pad + slot_index, -1)
        places = jnp.arange(group_rows, dtype=jnp.int32)
        return (places[:, None] == target[None, :]).astype(BF16)

    def by_expert(rows):
        return rows.reshape(expert_count, slot_pad, -1)

    placing = placing_of(expert_ids)
    send_grads = jnp.dot(placing, scaled_grad, preferred_element_type=F32).astype(BF16)
    send_rows = jnp.dot(placing, normed_mid, preferred_element_type=F32).astype(BF16)
    got_grads = exchange(by_expert(send_grads), "expert").reshape(group_rows, model_width)
    grad_blocks = gather_rel(got_grads, "tensor")
    input_blocks = gather_rel(layer_input, "tensor")
    send_rows, _ = lax.optimization_barrier((send_rows, got_grads))
    got_rows = exchange(by_expert(send_rows), "expert").reshape(group_rows, model_width)

    pre_blocks = []
    for shard_block in pick_rel(hidden_pre[0], tensor_at, tensor_count):
        block = jnp.pad(shard_block, ((0, 0), (0, slot_pad - slot_count), (0, 0)))
        pre_blocks.append(block.reshape(group_rows, unit_count))

    parts, pre_grads = [], []
    for grads, pre in zip(grad_blocks, pre_blocks):
        up_grad = contract_last(grads, outer_weight[0])
        pre_grad = jnp.where(pre > 0, up_grad, 0.0).astype(BF16)
        gate_part = jnp.sum(jnp.maximum(pre, 0).astype(F32) * up_grad, axis=1, keepdims=True)
        slot_part = contract_last(pre_grad, inner_weight[0])
        parts.append(jnp.concatenate([slot_part.astype(BF16), gate_part.astype(BF16)], axis=1))
        pre_grads.append(pre_grad)
    slot_sum = scatter_sum_rel(parts, "tensor", tensor_bits).astype(BF16)
    back_parts = pick_rel(by_expert(slot_sum), expert_at, expert_count)
    back_flat = jnp.concatenate(exchange_rel(back_parts, "expert"), axis=0)

    token_back = contract_first(placing_of(expert_ids ^ expert_at), back_flat)
    mid_grad = token_back[:, :model_width]
    gate_grad = token_back[:, model_width].astype(BF16)
    wide_residual = residual.astype(F32)
    gain_mid = jnp.sum(mid_grad * wide_residual * inv_mid, axis=0)
    resid_grad = out_grad.astype(F32) + norm_back(mid_grad, residual, inv_mid, expert_gain)
    resid_low = resid_grad.astype(BF16)

    seq_order = halving_order(tensor_bits)
    resid_blocks = gather_rel(resid_low, "tensor")
    piece = jnp.concatenate([resid_blocks[rel] for rel in seq_order], axis=0)

    def seq_rel(rows):
        blocks = rows.reshape((tensor_count, tok_rows) + rows.shape[1:])
        picked = pick_rel(blocks, tensor_at, tensor_count)
        return jnp.concatenate([picked[rel] for rel in seq_order], axis=0)

    query_rel, key_rel, value_rel, heads_rel, segments, positions = (
        seq_rel(rows)
        for rows in (
            query_rows,
            key_rows,
            value_rows,
            attn_heads,
            segment_ids,
            jnp.arange(tensor_count * tok_rows, dtype=jnp.int32),
        )
    )
    attend = softmax_transposed(query_rel, key_rel, positions, segments)

    share_rows = model_width // expert_count
    share_pad = -(-share_rows // 8) * 8

    def shares_of(rows, order):
        blocks = [
            jnp.pad(
                lax.dynamic_slice_in_dim(rows, (expert_at ^ rel) * share_rows, share_rows, 0),
                ((0, share_pad - share_rows), (0, 0)),
            )
            for rel in halving_order(order)
        ]
        return jnp.concatenate(blocks, axis=0)

    barrier = lax.optimization_barrier
    input_seq = jnp.concatenate([input_blocks[rel] for rel in seq_order], axis=0)
    input_seq, _ = barrier((input_seq, parts[-1]))
    unit_seq = input_seq.astype(F32) * inv_rms(input_seq)
    normed_cols = (unit_seq * attn_gain).astype(BF16).T
    pair_orders = [expert_bits, expert_bits[1:] + expert_bits[:1]]
    pair_shares = [shares_of(normed_cols, order) for order in pair_orders]
    piece, pair_shares = barrier((piece, pair_shares))

    head_grad = contract_last(piece, output_weight).astype(BF16)
    pair = 2 * DH
    backs, shares, normed_parts = [], [], 0.0
    for at in range(query_rows.shape[1] // pair):
        back_cols = attention_back(attend, query_rel, key_rel, value_rel, heads_rel, head_grad, at)
        which = at % len(pair_orders)
        shares.append(
            jnp.dot(pair_shares[which], back_cols, preferred_element_type=F32).astype(BF16)
        )
        backs.append(back_cols)
    backs, shares, got_rows = barrier((backs, shares, got_rows))
    orders = [pair_orders[at % len(pair_orders)] for at in range(len(shares))]
    sums = [halve_sum(part, "expert", order[:1]).astype(BF16) for part, order in zip(shares, orders)]
    for at, back_cols in enumerate(backs):
        for index, weight in enumerate((query_weight, key_weight, value_weight)):
            normed_parts = normed_parts + contract_last(
                back_cols[:, index * pair : (index + 1) * pair],
                weight[:, at * pair : (at + 1) * pair],
            )
    normed_grad = halve_sum(normed_parts.astype(BF16), "tensor", tensor_bits)
    gains = jnp.stack([jnp.sum(normed_parts * unit_seq, axis=0), gain_mid])
    gains = gains + flip(gains, "tensor", 1)

    sums, piece, grad_blocks = barrier((sums, piece, grad_blocks))
    flat_rows = jnp.concatenate(gather_rel(got_rows, "tensor"), axis=0)
    flat_grads = jnp.concatenate(grad_blocks, axis=0)
    active = jnp.maximum(jnp.concatenate(pre_blocks, axis=0), 0)
    inner_grad = contract_first(flat_rows, jnp.concatenate(pre_grads, axis=0)).astype(BF16)[None]
    outer_grad = contract_first(active, flat_grads).astype(BF16)[None]

    out_width = query_rows.shape[1]
    gain_size = 2 * model_width
    gain_rows = -(-gain_size // (8 * out_width)) * 8
    out_sum = contract_first(piece, heads_rel).astype(BF16)
    out_part = halve_sum(shares_of(out_sum, expert_bits), "expert", expert_bits[:1])

    def next_sums(sums, step):
        return [
            halve_sum(part.astype(BF16), "expert", [order[step]])
            for part, order in zip(sums, orders)
        ]

    last = len(expert_bits) - 1
    if last:
        sums = next_sums(sums, 1)
    sums, gains, out_part = barrier((sums, gains, out_part))
    for bit in tensor_bits[1:]:
        gains = gains + flip(gains, "tensor", 1 << bit)
    gains = gains + flip(gains, "expert", 1 << expert_bits[0])
    gains = jnp.pad(gains.reshape(gain_size), (0, gain_rows * out_width - gain_size))
    gains = gains.reshape(gain_rows, out_width)
    for step in range(1, last + 1):
        if step < last:
            sums = next_sums(sums, step + 1)
            out_part, sums[0] = barrier((out_part, sums[0]))
        else:
            out_part, inner_grad, normed_grad = barrier((out_part, inner_grad, normed_grad))
        out_part, gains = halve_with(out_part.astype(BF16), gains, "expert", expert_bits[step])
    out_part = out_part[:share_rows]
    weight_sums = [part[:share_rows] for part in sums]
    gains = gains.reshape(gain_rows * out_width)[:gain_size].reshape(2, model_width)
    query_part, key_part, value_part = (
        jnp.concatenate(
            [total[:, index * pair : (index + 1) * pair] for total in weight_sums], axis=1
        ).astype(BF16)
        for index in range(3)
    )

    inv_in = inv_rms(layer_input)
    input_grad = (resid_grad + norm_back(normed_grad, layer_input, inv_in, attn_gain)).astype(BF16)
    return (
        input_grad,
        gains[0],
        gains[1],
        query_part,
        key_part,
        value_part,
        out_part.astype(BF16).T,
        inner_grad,
        outer_grad,
        gate_grad,
    )


def solution(mesh):
    return jax.shard_map(
        shards,
        mesh=mesh,
        in_specs=(
            P(("expert", "tensor"), None),
            P(("expert", "tensor"), None),
            P(("expert", "tensor"), None),
            P(("expert", "tensor")),
            P(("expert", "tensor")),
            P(("expert", "tensor")),
            P("expert"),
            P("expert", "tensor"),
            P("expert", "tensor"),
            P("expert", "tensor"),
            P("expert", "tensor"),
            P(),
            P(),
            P(None, "tensor"),
            P(None, "tensor"),
            P(None, "tensor"),
            P("tensor", None),
            P("expert", None, "tensor"),
            P("expert", "tensor", None),
            P("expert", None, None, None, "tensor"),
        ),
        out_specs=(
            P(("expert", "tensor"), None),
            P(),
            P(),
            P("expert", "tensor"),
            P("expert", "tensor"),
            P("expert", "tensor"),
            P("tensor", "expert"),
            P("expert", None, "tensor"),
            P("expert", "tensor", None),
            P(("expert", "tensor")),
        ),
        check_vma=False,
    )
```

```python
import jax
import jax.numpy as jnp
from jax import lax
from jax.experimental import pallas as pl
from jax.experimental.pallas import tpu as pltpu
from jax.sharding import PartitionSpec as P

DH = 64


EPS = 1e-06

F32 = jnp.float32
BF16 = jnp.bfloat16

MOST_PERMUTES = 8


def inv_rms(row_data):
    wide_rows = row_data.astype(F32)
    return lax.rsqrt(jnp.mean(wide_rows * wide_rows, axis=-1, keepdims=True) + EPS)


def norm_back(grad_rows, row_data, inv_rows, gain_row):
    wide_rows = row_data.astype(F32)
    scaled = grad_rows * gain_row
    return inv_rows * (
        scaled
        - wide_rows * inv_rows * inv_rows * jnp.mean(scaled * wide_rows, axis=-1, keepdims=True)
    )


def contract_last(left, right):
    return lax.dot_general(left, right, (((1,), (1,)), ((), ())), preferred_element_type=F32)


def contract_first(left, right):
    return lax.dot_general(left, right, (((0,), (0,)), ((), ())), preferred_element_type=F32)


def flip(value, axis, mask):
    count = lax.axis_size(axis)
    return lax.ppermute(value, axis, [(at, at ^ mask) for at in range(count)])


def bits_of(axis):
    return lax.axis_size(axis).bit_length() - 1


def gather_rel(value, axis):
    held = {0: value}
    for bit in reversed(range(bits_of(axis))):
        for rel in list(held):
            held[rel | (1 << bit)] = flip(held[rel], axis, 1 << bit)
    return [held[rel] for rel in range(len(held))]


def pick_rel(blocks, index, count):
    return [lax.dynamic_index_in_dim(blocks, index ^ rel, 0, keepdims=False) for rel in range(count)]


def scatter_sum_rel(parts, axis, order):
    if len(parts) > MOST_PERMUTES:
        whole = jnp.stack(pick_rel(jnp.stack(parts), lax.axis_index(axis), len(parts)))
        return lax.psum_scatter(whole, axis, scatter_dimension=0, tiled=False).astype(F32)
    held = dict(enumerate(parts))
    for step, bit in enumerate(order):
        mask = 1 << bit
        last = step == len(order) - 1
        for rel in [r for r in held if r & mask]:
            got = flip(held.pop(rel), axis, mask)
            total = held[rel ^ mask].astype(F32) + got.astype(F32)
            held[rel ^ mask] = total if last else total.astype(BF16)
    return held[0]


def exchange_rel(parts, axis):
    count = len(parts)
    if count > MOST_PERMUTES:
        whole = jnp.stack(pick_rel(jnp.stack(parts), lax.axis_index(axis), count))
        whole = lax.all_to_all(whole, axis, split_axis=0, concat_axis=0, tiled=True)
        return pick_rel(whole, lax.axis_index(axis), count)
    got = {0: parts[0]}
    for rel in reversed(range(1, count)):
        got[rel] = flip(parts[rel], axis, rel)
    return [got[rel] for rel in range(count)]


def halving_order(order):
    places = 1 << len(order)
    last = len(order) - 1
    return [
        sum(((place >> (last - at)) & 1) << bit for at, bit in enumerate(order))
        for place in range(places)
    ]


def split_float(value):
    high = lax.reduce_precision(value, 8, 7)
    return jnp.concatenate([high.astype(BF16), (value - high).astype(BF16)], axis=0)


def halve_with(shares, extra, axis, bit):
    half = shares.shape[0] // 2
    rows = extra.shape[0]
    got = flip(jnp.concatenate([shares[half:], split_float(extra)], axis=0), axis, 1 << bit)
    high, low = got[half : half + rows].astype(F32), got[half + rows :].astype(F32)
    return shares[:half].astype(F32) + got[:half].astype(F32), extra + (high + low)


def halve_sum(shares, axis, order):
    for step, bit in enumerate(order):
        half = shares.shape[0] // 2
        got = flip(shares[half:], axis, 1 << bit)
        shares = shares[:half].astype(F32) + got.astype(F32)
        if step < len(order) - 1:
            shares = shares.astype(BF16)
    return shares


def exchange(blocks, axis):
    return lax.all_to_all(blocks, axis, split_axis=0, concat_axis=0, tiled=True)


def softmax_body(query_ref, key_ref, row_ref, col_ref, out_ref):
    position_q, segment_q = row_ref[0:1, :], row_ref[1:2, :]
    position_k, segment_k = col_ref[:, 0:1], col_ref[:, 1:2]
    allowed = (position_q >= position_k) & (segment_q == segment_k)
    for head in range(query_ref.shape[1] // DH):
        cols = slice(head * DH, head * DH + DH)
        scores = contract_last(key_ref[:, cols], query_ref[:, cols]) * (DH ** (-0.5))
        scores = jnp.where(allowed, scores, -jnp.inf)
        weights = jnp.exp(scores - jnp.max(scores, axis=0, keepdims=True))
        attend = weights / jnp.sum(weights, axis=0, keepdims=True)
        out_ref[head] = attend.astype(BF16)


def softmax_transposed(query_rows, key_rows, positions, segments):
    seq_rows, width = query_rows.shape
    pair = 2 * DH
    by_query = jnp.stack([positions, segments])
    return pl.pallas_call(
        softmax_body,
        grid=(width // pair,),
        in_specs=[
            pl.BlockSpec((seq_rows, pair), lambda at: (0, at)),
            pl.BlockSpec((seq_rows, pair), lambda at: (0, at)),
            pl.BlockSpec((2, seq_rows), lambda at: (0, 0)),
            pl.BlockSpec((seq_rows, 2), lambda at: (0, 0)),
        ],
        out_specs=pl.BlockSpec((2, seq_rows, seq_rows), lambda at: (at, 0, 0)),
        out_shape=jax.ShapeDtypeStruct((width // DH, seq_rows, seq_rows), BF16),
        compiler_params=pltpu.CompilerParams(vmem_limit_bytes=40 << 20),
        cost_estimate=pl.CostEstimate(
            flops=2 * width * seq_rows * seq_rows,
            transcendentals=width // DH * seq_rows * seq_rows,
            bytes_accessed=width // DH * seq_rows * seq_rows * 2,
        ),
    )(query_rows, key_rows, by_query, by_query.T)


def attention_body(attend_ref, query_ref, key_ref, value_ref, heads_ref, grad_ref, out_ref):
    width = query_ref.shape[1]
    products = grad_ref[...].astype(F32) * heads_ref[...].astype(F32)
    products = products.T
    for head in range(width // DH):
        cols = slice(head * DH, head * DH + DH)
        row_dot = jnp.sum(products[cols], axis=0, keepdims=True)
        attend = attend_ref[head]
        grads = grad_ref[:, cols]
        attend_grad = contract_last(value_ref[:, cols], grads)
        score_grad = attend.astype(F32) * (attend_grad - row_dot) * (DH ** (-0.5))
        score_grad = score_grad.astype(BF16)
        for at, back in enumerate(
            (
                contract_first(score_grad, key_ref[:, cols]),
                jnp.dot(score_grad, query_ref[:, cols], preferred_element_type=F32),
                jnp.dot(attend, grads, preferred_element_type=F32),
            )
        ):
            low = at * width + head * DH
            out_ref[:, low : low + DH] = back.astype(BF16)


def attention_back(attend, query_rows, key_rows, value_rows, attn_heads, head_grad, pair_at):
    seq_rows = query_rows.shape[0]
    pair = 2 * DH
    cols = pl.BlockSpec((seq_rows, pair), lambda at: (0, pair_at))
    return pl.pallas_call(
        attention_body,
        grid=(1,),
        in_specs=[
            pl.BlockSpec((2, seq_rows, seq_rows), lambda at: (pair_at, 0, 0)),
            cols,
            cols,
            cols,
            cols,
            cols,
        ],
        out_specs=pl.BlockSpec((seq_rows, 3 * pair), lambda at: (0, 0)),
        out_shape=jax.ShapeDtypeStruct((seq_rows, 3 * pair), BF16),
        compiler_params=pltpu.CompilerParams(vmem_limit_bytes=40 << 20),
        cost_estimate=pl.CostEstimate(
            flops=8 * pair * seq_rows * seq_rows,
            transcendentals=0,
            bytes_accessed=4 * seq_rows * seq_rows + 16 * pair * seq_rows,
        ),
    )(attend, query_rows, key_rows, value_rows, attn_heads, head_grad)


def shards(
    layer_input,
    residual,
    out_grad,
    gate_prob,
    expert_ids,
    slot_index,
    segment_ids,
    query_rows,
    key_rows,
    value_rows,
    attn_heads,
    attn_gain,
    expert_gain,
    query_weight,
    key_weight,
    value_weight,
    output_weight,
    inner_weight,
    outer_weight,
    hidden_pre,
):
    tensor_count = lax.axis_size("tensor")
    expert_count = lax.axis_size("expert")
    tensor_at = lax.axis_index("tensor")
    expert_at = lax.axis_index("expert")
    tok_rows, model_width = layer_input.shape
    slot_count = hidden_pre.shape[3]
    unit_count = hidden_pre.shape[4]
    slot_pad = -(-slot_count // 8) * 8
    group_rows = expert_count * slot_pad

    tensor_bits = list(range(bits_of("tensor")))
    expert_bits = list(range(bits_of("expert")))

    inv_mid = inv_rms(residual)
    normed_mid = (residual.astype(F32) * inv_mid * expert_gain).astype(BF16)
    scaled_grad = (gate_prob[:, None] * out_grad.astype(F32)).astype(BF16)

    def placing_of(experts):
        target = jnp.where(slot_index >= 0, experts * slot_pad + slot_index, -1)
        places = jnp.arange(group_rows, dtype=jnp.int32)
        return (places[:, None] == target[None, :]).astype(BF16)

    def by_expert(rows):
        return rows.reshape(expert_count, slot_pad, -1)

    placing = placing_of(expert_ids)
    send_grads = jnp.dot(placing, scaled_grad, preferred_element_type=F32).astype(BF16)
    send_rows = jnp.dot(placing, normed_mid, preferred_element_type=F32).astype(BF16)
    got_grads = exchange(by_expert(send_grads), "expert").reshape(group_rows, model_width)
    grad_blocks = gather_rel(got_grads, "tensor")
    input_blocks = gather_rel(layer_input, "tensor")
    send_rows, _ = lax.optimization_barrier((send_rows, got_grads))
    got_rows = exchange(by_expert(send_rows), "expert").reshape(group_rows, model_width)

    pre_blocks = []
    for shard_block in pick_rel(hidden_pre[0], tensor_at, tensor_count):
        block = jnp.pad(shard_block, ((0, 0), (0, slot_pad - slot_count), (0, 0)))
        pre_blocks.append(block.reshape(group_rows, unit_count))

    parts, pre_grads = [], []
    for grads, pre in zip(grad_blocks, pre_blocks):
        up_grad = contract_last(grads, outer_weight[0])
        pre_grad = jnp.where(pre > 0, up_grad, 0.0).astype(BF16)
        gate_part = jnp.sum(jnp.maximum(pre, 0).astype(F32) * up_grad, axis=1, keepdims=True)
        slot_part = contract_last(pre_grad, inner_weight[0])
        parts.append(jnp.concatenate([slot_part.astype(BF16), gate_part.astype(BF16)], axis=1))
        pre_grads.append(pre_grad)
    slot_sum = scatter_sum_rel(parts, "tensor", tensor_bits).astype(BF16)
    back_parts = pick_rel(by_expert(slot_sum), expert_at, expert_count)
    back_flat = jnp.concatenate(exchange_rel(back_parts, "expert"), axis=0)

    token_back = contract_first(placing_of(expert_ids ^ expert_at), back_flat)
    mid_grad = token_back[:, :model_width]
    gate_grad = token_back[:, model_width].astype(BF16)
    wide_residual = residual.astype(F32)
    gain_mid = jnp.sum(mid_grad * wide_residual * inv_mid, axis=0)
    resid_grad = out_grad.astype(F32) + norm_back(mid_grad, residual, inv_mid, expert_gain)
    resid_low = resid_grad.astype(BF16)

    seq_order = halving_order(tensor_bits)
    resid_blocks = gather_rel(resid_low, "tensor")
    piece = jnp.concatenate([resid_blocks[rel] for rel in seq_order], axis=0)

    def seq_rel(rows):
        blocks = rows.reshape((tensor_count, tok_rows) + rows.shape[1:])
        picked = pick_rel(blocks, tensor_at, tensor_count)
        return jnp.concatenate([picked[rel] for rel in seq_order], axis=0)

    query_rel, key_rel, value_rel, heads_rel, segments, positions = (
        seq_rel(rows)
        for rows in (
            query_rows,
            key_rows,
            value_rows,
            attn_heads,
            segment_ids,
            jnp.arange(tensor_count * tok_rows, dtype=jnp.int32),
        )
    )
    attend = softmax_transposed(query_rel, key_rel, positions, segments)

    share_rows = model_width // expert_count
    share_pad = -(-share_rows // 8) * 8

    def shares_of(rows, order):
        blocks = [
            jnp.pad(
                lax.dynamic_slice_in_dim(rows, (expert_at ^ rel) * share_rows, share_rows, 0),
                ((0, share_pad - share_rows), (0, 0)),
            )
            for rel in halving_order(order)
        ]
        return jnp.concatenate(blocks, axis=0)

    barrier = lax.optimization_barrier
    input_seq = jnp.concatenate([input_blocks[rel] for rel in seq_order], axis=0)
    input_seq, _ = barrier((input_seq, parts[-1]))
    unit_seq = input_seq.astype(F32) * inv_rms(input_seq)
    normed_cols = (unit_seq * attn_gain).astype(BF16).T
    pair_orders = [expert_bits, expert_bits[1:] + expert_bits[:1]]
    pair_shares = [shares_of(normed_cols, order) for order in pair_orders]
    piece, pair_shares = barrier((piece, pair_shares))

    head_grad = contract_last(piece, output_weight).astype(BF16)
    pair = 2 * DH
    backs, shares, normed_parts = [], [], 0.0
    for at in range(query_rows.shape[1] // pair):
        back_cols = attention_back(attend, query_rel, key_rel, value_rel, heads_rel, head_grad, at)
        which = at % len(pair_orders)
        shares.append(
            jnp.dot(pair_shares[which], back_cols, preferred_element_type=F32).astype(BF16)
        )
        backs.append(back_cols)
    backs, shares, got_rows = barrier((backs, shares, got_rows))
    orders = [pair_orders[at % len(pair_orders)] for at in range(len(shares))]
    sums = [halve_sum(part, "expert", order[:1]).astype(BF16) for part, order in zip(shares, orders)]
    for at, back_cols in enumerate(backs):
        for index, weight in enumerate((query_weight, key_weight, value_weight)):
            normed_parts = normed_parts + contract_last(
                back_cols[:, index * pair : (index + 1) * pair],
                weight[:, at * pair : (at + 1) * pair],
            )
    normed_half = halve_sum(normed_parts.astype(BF16), "tensor", tensor_bits[:1])
    gains = jnp.stack([jnp.sum(normed_parts * unit_seq, axis=0), gain_mid])
    gains = gains + flip(gains, "tensor", 1)

    sums, piece, grad_blocks = barrier((sums, piece, grad_blocks))
    flat_rows = jnp.concatenate(gather_rel(got_rows, "tensor"), axis=0)
    flat_grads = jnp.concatenate(grad_blocks, axis=0)
    active = jnp.maximum(jnp.concatenate(pre_blocks, axis=0), 0)
    inner_grad = contract_first(flat_rows, jnp.concatenate(pre_grads, axis=0)).astype(BF16)[None]
    outer_grad = contract_first(active, flat_grads).astype(BF16)[None]

    out_width = query_rows.shape[1]
    gain_size = 2 * model_width
    gain_rows = -(-gain_size // (8 * out_width)) * 8
    out_sum = contract_first(piece, heads_rel).astype(BF16)
    out_part = halve_sum(shares_of(out_sum, expert_bits), "expert", expert_bits[:1])

    def next_sums(sums, step):
        return [
            halve_sum(part.astype(BF16), "expert", [order[step]])
            for part, order in zip(sums, orders)
        ]

    last = len(expert_bits) - 1
    if last:
        sums = next_sums(sums, 1)
    sums, gains, out_part, normed_half, outer_grad = barrier(
        (sums, gains, out_part, normed_half, outer_grad)
    )
    normed_grad = halve_sum(normed_half.astype(BF16), "tensor", tensor_bits[1:]).astype(F32)
    for bit in tensor_bits[1:]:
        gains = gains + flip(gains, "tensor", 1 << bit)
    gains = gains + flip(gains, "expert", 1 << expert_bits[0])
    gains = jnp.pad(gains.reshape(gain_size), (0, gain_rows * out_width - gain_size))
    gains = gains.reshape(gain_rows, out_width)
    for step in range(2, last + 1):
        sums = next_sums(sums, step)
    for step in range(1, last + 1):
        if step == last:
            out_part, sums[0], normed_grad, inner_grad = barrier(
                (out_part, sums[0], normed_grad, inner_grad)
            )
        out_part, gains = halve_with(out_part.astype(BF16), gains, "expert", expert_bits[step])
    out_part = out_part[:share_rows]
    weight_sums = [part[:share_rows] for part in sums]
    gains = gains.reshape(gain_rows * out_width)[:gain_size].reshape(2, model_width)
    query_part, key_part, value_part = (
        jnp.concatenate(
            [total[:, index * pair : (index + 1) * pair] for total in weight_sums], axis=1
        ).astype(BF16)
        for index in range(3)
    )

    inv_in = inv_rms(layer_input)
    input_grad = (resid_grad + norm_back(normed_grad, layer_input, inv_in, attn_gain)).astype(BF16)
    return (
        input_grad,
        gains[0],
        gains[1],
        query_part,
        key_part,
        value_part,
        out_part.astype(BF16).T,
        inner_grad,
        outer_grad,
        gate_grad,
    )


def solution(mesh):
    return jax.shard_map(
        shards,
        mesh=mesh,
        in_specs=(
            P(("expert", "tensor"), None),
            P(("expert", "tensor"), None),
            P(("expert", "tensor"), None),
            P(("expert", "tensor")),
            P(("expert", "tensor")),
            P(("expert", "tensor")),
            P("expert"),
            P("expert", "tensor"),
            P("expert", "tensor"),
            P("expert", "tensor"),
            P("expert", "tensor"),
            P(),
            P(),
            P(None, "tensor"),
            P(None, "tensor"),
            P(None, "tensor"),
            P("tensor", None),
            P("expert", None, "tensor"),
            P("expert", "tensor", None),
            P("expert", None, None, None, "tensor"),
        ),
        out_specs=(
            P(("expert", "tensor"), None),
            P(),
            P(),
            P("expert", "tensor"),
            P("expert", "tensor"),
            P("expert", "tensor"),
            P("tensor", "expert"),
            P("expert", None, "tensor"),
            P("expert", "tensor", None),
            P(("expert", "tensor")),
        ),
        check_vma=False,
    )
```

```python
import jax
import jax.numpy as jnp
from jax import lax
from jax.experimental import pallas as pl
from jax.experimental.pallas import tpu as pltpu
from jax.sharding import PartitionSpec as P

DH = 64


EPS = 1e-06

F32 = jnp.float32
BF16 = jnp.bfloat16

MOST_PERMUTES = 8


def inv_rms(row_data):
    wide_rows = row_data.astype(F32)
    return lax.rsqrt(jnp.mean(wide_rows * wide_rows, axis=-1, keepdims=True) + EPS)


def norm_back(grad_rows, row_data, inv_rows, gain_row):
    wide_rows = row_data.astype(F32)
    scaled = grad_rows * gain_row
    return inv_rows * (
        scaled
        - wide_rows * inv_rows * inv_rows * jnp.mean(scaled * wide_rows, axis=-1, keepdims=True)
    )


def contract_last(left, right):
    return lax.dot_general(left, right, (((1,), (1,)), ((), ())), preferred_element_type=F32)


def contract_first(left, right):
    return lax.dot_general(left, right, (((0,), (0,)), ((), ())), preferred_element_type=F32)


def flip(value, axis, mask):
    count = lax.axis_size(axis)
    return lax.ppermute(value, axis, [(at, at ^ mask) for at in range(count)])


def bits_of(axis):
    return lax.axis_size(axis).bit_length() - 1


def gather_rel(value, axis):
    held = {0: value}
    for bit in reversed(range(bits_of(axis))):
        for rel in list(held):
            held[rel | (1 << bit)] = flip(held[rel], axis, 1 << bit)
    return [held[rel] for rel in range(len(held))]


def pick_rel(blocks, index, count):
    return [lax.dynamic_index_in_dim(blocks, index ^ rel, 0, keepdims=False) for rel in range(count)]


def scatter_sum_rel(parts, axis, order):
    if len(parts) > MOST_PERMUTES:
        whole = jnp.stack(pick_rel(jnp.stack(parts), lax.axis_index(axis), len(parts)))
        return lax.psum_scatter(whole, axis, scatter_dimension=0, tiled=False).astype(F32)
    held = dict(enumerate(parts))
    for step, bit in enumerate(order):
        mask = 1 << bit
        last = step == len(order) - 1
        for rel in [r for r in held if r & mask]:
            got = flip(held.pop(rel), axis, mask)
            total = held[rel ^ mask].astype(F32) + got.astype(F32)
            held[rel ^ mask] = total if last else total.astype(BF16)
    return held[0]


def exchange_rel(parts, axis):
    count = len(parts)
    if count > MOST_PERMUTES:
        whole = jnp.stack(pick_rel(jnp.stack(parts), lax.axis_index(axis), count))
        whole = lax.all_to_all(whole, axis, split_axis=0, concat_axis=0, tiled=True)
        return pick_rel(whole, lax.axis_index(axis), count)
    got = {0: parts[0]}
    for rel in reversed(range(1, count)):
        got[rel] = flip(parts[rel], axis, rel)
    return [got[rel] for rel in range(count)]


def halving_order(order):
    places = 1 << len(order)
    last = len(order) - 1
    return [
        sum(((place >> (last - at)) & 1) << bit for at, bit in enumerate(order))
        for place in range(places)
    ]


def halve_sum(shares, axis, order):
    for step, bit in enumerate(order):
        half = shares.shape[0] // 2
        got = flip(shares[half:], axis, 1 << bit)
        shares = shares[:half].astype(F32) + got.astype(F32)
        if step < len(order) - 1:
            shares = shares.astype(BF16)
    return shares


def exchange(blocks, axis):
    return lax.all_to_all(blocks, axis, split_axis=0, concat_axis=0, tiled=True)


def softmax_body(query_ref, key_ref, row_ref, col_ref, out_ref):
    position_q, segment_q = row_ref[0:1, :], row_ref[1:2, :]
    position_k, segment_k = col_ref[:, 0:1], col_ref[:, 1:2]
    allowed = (position_q >= position_k) & (segment_q == segment_k)
    for head in range(query_ref.shape[1] // DH):
        cols = slice(head * DH, head * DH + DH)
        scores = contract_last(key_ref[:, cols], query_ref[:, cols]) * (DH ** (-0.5))
        scores = jnp.where(allowed, scores, -jnp.inf)
        weights = jnp.exp(scores - jnp.max(scores, axis=0, keepdims=True))
        attend = weights / jnp.sum(weights, axis=0, keepdims=True)
        out_ref[head] = attend.astype(BF16)


def softmax_transposed(query_rows, key_rows, positions, segments):
    seq_rows, width = query_rows.shape
    pair = 2 * DH
    by_query = jnp.stack([positions, segments])
    return pl.pallas_call(
        softmax_body,
        grid=(width // pair,),
        in_specs=[
            pl.BlockSpec((seq_rows, pair), lambda at: (0, at)),
            pl.BlockSpec((seq_rows, pair), lambda at: (0, at)),
            pl.BlockSpec((2, seq_rows), lambda at: (0, 0)),
            pl.BlockSpec((seq_rows, 2), lambda at: (0, 0)),
        ],
        out_specs=pl.BlockSpec((2, seq_rows, seq_rows), lambda at: (at, 0, 0)),
        out_shape=jax.ShapeDtypeStruct((width // DH, seq_rows, seq_rows), BF16),
        compiler_params=pltpu.CompilerParams(vmem_limit_bytes=40 << 20),
        cost_estimate=pl.CostEstimate(
            flops=2 * width * seq_rows * seq_rows,
            transcendentals=width // DH * seq_rows * seq_rows,
            bytes_accessed=width // DH * seq_rows * seq_rows * 2,
        ),
    )(query_rows, key_rows, by_query, by_query.T)


def attention_body(attend_ref, query_ref, key_ref, value_ref, heads_ref, grad_ref, out_ref):
    width = query_ref.shape[1]
    products = grad_ref[...].astype(F32) * heads_ref[...].astype(F32)
    products = products.T
    for head in range(width // DH):
        cols = slice(head * DH, head * DH + DH)
        row_dot = jnp.sum(products[cols], axis=0, keepdims=True)
        attend = attend_ref[head]
        grads = grad_ref[:, cols]
        attend_grad = contract_last(value_ref[:, cols], grads)
        score_grad = attend.astype(F32) * (attend_grad - row_dot) * (DH ** (-0.5))
        score_grad = score_grad.astype(BF16)
        for at, back in enumerate(
            (
                contract_first(score_grad, key_ref[:, cols]),
                jnp.dot(score_grad, query_ref[:, cols], preferred_element_type=F32),
                jnp.dot(attend, grads, preferred_element_type=F32),
            )
        ):
            low = at * width + head * DH
            out_ref[:, low : low + DH] = back.astype(BF16)


def attention_back(attend, query_rows, key_rows, value_rows, attn_heads, head_grad, pair_at):
    seq_rows = query_rows.shape[0]
    pair = 2 * DH
    cols = pl.BlockSpec((seq_rows, pair), lambda at: (0, pair_at))
    return pl.pallas_call(
        attention_body,
        grid=(1,),
        in_specs=[
            pl.BlockSpec((2, seq_rows, seq_rows), lambda at: (pair_at, 0, 0)),
            cols,
            cols,
            cols,
            cols,
            cols,
        ],
        out_specs=pl.BlockSpec((seq_rows, 3 * pair), lambda at: (0, 0)),
        out_shape=jax.ShapeDtypeStruct((seq_rows, 3 * pair), BF16),
        compiler_params=pltpu.CompilerParams(vmem_limit_bytes=40 << 20),
        cost_estimate=pl.CostEstimate(
            flops=8 * pair * seq_rows * seq_rows,
            transcendentals=0,
            bytes_accessed=4 * seq_rows * seq_rows + 16 * pair * seq_rows,
        ),
    )(attend, query_rows, key_rows, value_rows, attn_heads, head_grad)


def shards(
    layer_input,
    residual,
    out_grad,
    gate_prob,
    expert_ids,
    slot_index,
    segment_ids,
    query_rows,
    key_rows,
    value_rows,
    attn_heads,
    attn_gain,
    expert_gain,
    query_weight,
    key_weight,
    value_weight,
    output_weight,
    inner_weight,
    outer_weight,
    hidden_pre,
):
    tensor_count = lax.axis_size("tensor")
    expert_count = lax.axis_size("expert")
    tensor_at = lax.axis_index("tensor")
    expert_at = lax.axis_index("expert")
    tok_rows, model_width = layer_input.shape
    slot_count = hidden_pre.shape[3]
    unit_count = hidden_pre.shape[4]
    slot_pad = -(-slot_count // 8) * 8
    group_rows = expert_count * slot_pad

    tensor_bits = list(range(bits_of("tensor")))
    expert_bits = list(range(bits_of("expert")))

    inv_mid = inv_rms(residual)
    normed_mid = (residual.astype(F32) * inv_mid * expert_gain).astype(BF16)
    scaled_grad = (gate_prob[:, None] * out_grad.astype(F32)).astype(BF16)

    def placing_of(experts):
        target = jnp.where(slot_index >= 0, experts * slot_pad + slot_index, -1)
        places = jnp.arange(group_rows, dtype=jnp.int32)
        return (places[:, None] == target[None, :]).astype(BF16)

    def by_expert(rows):
        return rows.reshape(expert_count, slot_pad, -1)

    placing = placing_of(expert_ids)
    send_grads = jnp.dot(placing, scaled_grad, preferred_element_type=F32).astype(BF16)
    send_rows = jnp.dot(placing, normed_mid, preferred_element_type=F32).astype(BF16)
    got_grads = exchange(by_expert(send_grads), "expert").reshape(group_rows, model_width)
    grad_blocks = gather_rel(got_grads, "tensor")
    input_blocks = gather_rel(layer_input, "tensor")
    send_rows, _ = lax.optimization_barrier((send_rows, got_grads))
    got_rows = exchange(by_expert(send_rows), "expert").reshape(group_rows, model_width)

    pre_blocks = []
    for shard_block in pick_rel(hidden_pre[0], tensor_at, tensor_count):
        block = jnp.pad(shard_block, ((0, 0), (0, slot_pad - slot_count), (0, 0)))
        pre_blocks.append(block.reshape(group_rows, unit_count))

    parts, pre_grads = [], []
    for grads, pre in zip(grad_blocks, pre_blocks):
        up_grad = contract_last(grads, outer_weight[0])
        pre_grad = jnp.where(pre > 0, up_grad, 0.0).astype(BF16)
        gate_part = jnp.sum(jnp.maximum(pre, 0).astype(F32) * up_grad, axis=1, keepdims=True)
        slot_part = contract_last(pre_grad, inner_weight[0])
        parts.append(jnp.concatenate([slot_part.astype(BF16), gate_part.astype(BF16)], axis=1))
        pre_grads.append(pre_grad)
    slot_sum = scatter_sum_rel(parts, "tensor", tensor_bits).astype(BF16)
    back_parts = pick_rel(by_expert(slot_sum), expert_at, expert_count)
    back_flat = jnp.concatenate(exchange_rel(back_parts, "expert"), axis=0)

    token_back = contract_first(placing_of(expert_ids ^ expert_at), back_flat)
    mid_grad = token_back[:, :model_width]
    gate_grad = token_back[:, model_width].astype(BF16)
    wide_residual = residual.astype(F32)
    gain_mid = jnp.sum(mid_grad * wide_residual * inv_mid, axis=0)
    resid_grad = out_grad.astype(F32) + norm_back(mid_grad, residual, inv_mid, expert_gain)
    resid_low = resid_grad.astype(BF16)

    seq_order = halving_order(tensor_bits)
    resid_blocks = gather_rel(resid_low, "tensor")
    piece = jnp.concatenate([resid_blocks[rel] for rel in seq_order], axis=0)

    def seq_rel(rows):
        blocks = rows.reshape((tensor_count, tok_rows) + rows.shape[1:])
        picked = pick_rel(blocks, tensor_at, tensor_count)
        return jnp.concatenate([picked[rel] for rel in seq_order], axis=0)

    query_rel, key_rel, value_rel, heads_rel, segments, positions = (
        seq_rel(rows)
        for rows in (
            query_rows,
            key_rows,
            value_rows,
            attn_heads,
            segment_ids,
            jnp.arange(tensor_count * tok_rows, dtype=jnp.int32),
        )
    )
    attend = softmax_transposed(query_rel, key_rel, positions, segments)

    share_rows = model_width // expert_count
    share_pad = -(-share_rows // 8) * 8

    def shares_of(rows, order):
        blocks = [
            jnp.pad(
                lax.dynamic_slice_in_dim(rows, (expert_at ^ rel) * share_rows, share_rows, 0),
                ((0, share_pad - share_rows), (0, 0)),
            )
            for rel in halving_order(order)
        ]
        return jnp.concatenate(blocks, axis=0)

    barrier = lax.optimization_barrier
    input_seq = jnp.concatenate([input_blocks[rel] for rel in seq_order], axis=0)
    input_seq, _ = barrier((input_seq, parts[-1]))
    unit_seq = input_seq.astype(F32) * inv_rms(input_seq)
    normed_cols = (unit_seq * attn_gain).astype(BF16).T
    pair_orders = [expert_bits, expert_bits[1:2] + expert_bits[:1] + expert_bits[2:]]
    pair_shares = [shares_of(normed_cols, order) for order in pair_orders]
    piece, pair_shares = barrier((piece, pair_shares))

    head_grad = contract_last(piece, output_weight).astype(BF16)
    pair = 2 * DH
    backs, shares, normed_parts = [], [], 0.0
    for at in range(query_rows.shape[1] // pair):
        back_cols = attention_back(attend, query_rel, key_rel, value_rel, heads_rel, head_grad, at)
        which = at % len(pair_orders)
        shares.append(
            jnp.dot(pair_shares[which], back_cols, preferred_element_type=F32).astype(BF16)
        )
        backs.append(back_cols)
    backs, shares, got_rows = barrier((backs, shares, got_rows))
    orders = [pair_orders[at % len(pair_orders)] for at in range(len(shares))]

    def next_sums(sums, step, other):
        halves = [part.shape[0] // 2 for part in sums]
        got = [
            flip(part[half:].astype(BF16), "expert", 1 << order[step])
            for part, half, order in zip(sums, halves, orders)
        ]
        got, other = barrier((got, other))
        sums = [part[:half].astype(F32) + block.astype(F32) for part, half, block in zip(sums, halves, got)]
        if step < len(expert_bits) - 1:
            sums = [part.astype(BF16) for part in sums]
        return sums, other

    sums, piece = next_sums(shares, 0, piece)
    for at, back_cols in enumerate(backs):
        for index, weight in enumerate((query_weight, key_weight, value_weight)):
            normed_parts = normed_parts + contract_last(
                back_cols[:, index * pair : (index + 1) * pair],
                weight[:, at * pair : (at + 1) * pair],
            )
    normed_grad = halve_sum(normed_parts.astype(BF16), "tensor", tensor_bits)
    gains = jnp.stack([jnp.sum(normed_parts * unit_seq, axis=0), gain_mid])

    sums, piece = barrier((sums, piece))
    flat_rows = jnp.concatenate(gather_rel(got_rows, "tensor"), axis=0)
    active = jnp.maximum(jnp.concatenate(pre_blocks, axis=0), 0)
    inner_grad = contract_first(flat_rows, jnp.concatenate(pre_grads, axis=0)).astype(BF16)[None]

    out_sum = contract_first(piece, heads_rel).astype(BF16)
    out_shares = shares_of(out_sum, expert_bits)

    if len(expert_bits) > 1:
        sums, out_shares = next_sums(sums, 1, out_shares)
    sums, out_shares, gains = barrier((sums, out_shares, gains))
    for bit in tensor_bits:
        gains = gains + flip(gains, "tensor", 1 << bit)
    out_half = out_shares.shape[0] // 2
    out_got = flip(out_shares[out_half:], "expert", 1 << expert_bits[0])
    for step in range(2, len(expert_bits)):
        sums, out_got = next_sums(sums, step, out_got)
    out_part = (out_shares[:out_half].astype(F32) + out_got.astype(F32)).astype(BF16)
    sums, out_part, gains = barrier((sums, out_part, gains))
    for bit in expert_bits:
        gains = gains + flip(gains, "expert", 1 << bit)
    for step in range(1, len(expert_bits)):
        if step == len(expert_bits) - 1:
            out_part, inner_grad, normed_grad, grad_blocks = barrier(
                (out_part, inner_grad, normed_grad, grad_blocks)
            )
        out_part = halve_sum(out_part.astype(BF16), "expert", [expert_bits[step]])
    out_part = out_part[:share_rows]
    weight_sums = [part[:share_rows] for part in sums]
    flat_grads = jnp.concatenate(grad_blocks, axis=0)
    outer_grad = contract_first(active, flat_grads).astype(BF16)[None]
    query_part, key_part, value_part = (
        jnp.concatenate(
            [total[:, index * pair : (index + 1) * pair] for total in weight_sums], axis=1
        ).astype(BF16)
        for index in range(3)
    )

    inv_in = inv_rms(layer_input)
    input_grad = (resid_grad + norm_back(normed_grad, layer_input, inv_in, attn_gain)).astype(BF16)
    return (
        input_grad,
        gains[0],
        gains[1],
        query_part,
        key_part,
        value_part,
        out_part.astype(BF16).T,
        inner_grad,
        outer_grad,
        gate_grad,
    )


def solution(mesh):
    return jax.shard_map(
        shards,
        mesh=mesh,
        in_specs=(
            P(("expert", "tensor"), None),
            P(("expert", "tensor"), None),
            P(("expert", "tensor"), None),
            P(("expert", "tensor")),
            P(("expert", "tensor")),
            P(("expert", "tensor")),
            P("expert"),
            P("expert", "tensor"),
            P("expert", "tensor"),
            P("expert", "tensor"),
            P("expert", "tensor"),
            P(),
            P(),
            P(None, "tensor"),
            P(None, "tensor"),
            P(None, "tensor"),
            P("tensor", None),
            P("expert", None, "tensor"),
            P("expert", "tensor", None),
            P("expert", None, None, None, "tensor"),
        ),
        out_specs=(
            P(("expert", "tensor"), None),
            P(),
            P(),
            P("expert", "tensor"),
            P("expert", "tensor"),
            P("expert", "tensor"),
            P("tensor", "expert"),
            P("expert", None, "tensor"),
            P("expert", "tensor", None),
            P(("expert", "tensor")),
        ),
        check_vma=False,
    )
```

```python
import jax
import jax.numpy as jnp
from jax import lax
from jax.experimental import pallas as pl
from jax.experimental.pallas import tpu as pltpu
from jax.sharding import PartitionSpec as P

DH = 64


EPS = 1e-06

F32 = jnp.float32
BF16 = jnp.bfloat16

MOST_PERMUTES = 8


def inv_rms(row_data):
    wide_rows = row_data.astype(F32)
    return lax.rsqrt(jnp.mean(wide_rows * wide_rows, axis=-1, keepdims=True) + EPS)


def norm_back(grad_rows, row_data, inv_rows, gain_row):
    wide_rows = row_data.astype(F32)
    scaled = grad_rows * gain_row
    return inv_rows * (
        scaled
        - wide_rows * inv_rows * inv_rows * jnp.mean(scaled * wide_rows, axis=-1, keepdims=True)
    )


def contract_last(left, right):
    return lax.dot_general(left, right, (((1,), (1,)), ((), ())), preferred_element_type=F32)


def contract_first(left, right):
    return lax.dot_general(left, right, (((0,), (0,)), ((), ())), preferred_element_type=F32)


def flip(value, axis, mask):
    count = lax.axis_size(axis)
    return lax.ppermute(value, axis, [(at, at ^ mask) for at in range(count)])


def bits_of(axis):
    return lax.axis_size(axis).bit_length() - 1


def gather_rel(value, axis):
    held = {0: value}
    for bit in reversed(range(bits_of(axis))):
        for rel in list(held):
            held[rel | (1 << bit)] = flip(held[rel], axis, 1 << bit)
    return [held[rel] for rel in range(len(held))]


def pick_rel(blocks, index, count):
    return [lax.dynamic_index_in_dim(blocks, index ^ rel, 0, keepdims=False) for rel in range(count)]


def scatter_sum_rel(parts, axis, order):
    if len(parts) > MOST_PERMUTES:
        whole = jnp.stack(pick_rel(jnp.stack(parts), lax.axis_index(axis), len(parts)))
        return lax.psum_scatter(whole, axis, scatter_dimension=0, tiled=False).astype(F32)
    held = dict(enumerate(parts))
    for step, bit in enumerate(order):
        mask = 1 << bit
        last = step == len(order) - 1
        for rel in [r for r in held if r & mask]:
            got = flip(held.pop(rel), axis, mask)
            total = held[rel ^ mask].astype(F32) + got.astype(F32)
            held[rel ^ mask] = total if last else total.astype(BF16)
    return held[0]


def exchange_rel(parts, axis):
    count = len(parts)
    if count > MOST_PERMUTES:
        whole = jnp.stack(pick_rel(jnp.stack(parts), lax.axis_index(axis), count))
        whole = lax.all_to_all(whole, axis, split_axis=0, concat_axis=0, tiled=True)
        return pick_rel(whole, lax.axis_index(axis), count)
    got = {0: parts[0]}
    for rel in reversed(range(1, count)):
        got[rel] = flip(parts[rel], axis, rel)
    return [got[rel] for rel in range(count)]


def halving_order(order):
    places = 1 << len(order)
    last = len(order) - 1
    return [
        sum(((place >> (last - at)) & 1) << bit for at, bit in enumerate(order))
        for place in range(places)
    ]


def halve_sum(shares, axis, order):
    for step, bit in enumerate(order):
        half = shares.shape[0] // 2
        got = flip(shares[half:], axis, 1 << bit)
        shares = shares[:half].astype(F32) + got.astype(F32)
        if step < len(order) - 1:
            shares = shares.astype(BF16)
    return shares


def exchange(blocks, axis):
    return lax.all_to_all(blocks, axis, split_axis=0, concat_axis=0, tiled=True)


def softmax_body(query_ref, key_ref, row_ref, col_ref, out_ref):
    position_q, segment_q = row_ref[0:1, :], row_ref[1:2, :]
    position_k, segment_k = col_ref[:, 0:1], col_ref[:, 1:2]
    allowed = (position_q >= position_k) & (segment_q == segment_k)
    for head in range(query_ref.shape[1] // DH):
        cols = slice(head * DH, head * DH + DH)
        scores = contract_last(key_ref[:, cols], query_ref[:, cols]) * (DH ** (-0.5))
        scores = jnp.where(allowed, scores, -jnp.inf)
        weights = jnp.exp(scores - jnp.max(scores, axis=0, keepdims=True))
        attend = weights / jnp.sum(weights, axis=0, keepdims=True)
        out_ref[head] = attend.astype(BF16)


def softmax_transposed(query_rows, key_rows, positions, segments):
    seq_rows, width = query_rows.shape
    pair = 2 * DH
    by_query = jnp.stack([positions, segments])
    return pl.pallas_call(
        softmax_body,
        grid=(width // pair,),
        in_specs=[
            pl.BlockSpec((seq_rows, pair), lambda at: (0, at)),
            pl.BlockSpec((seq_rows, pair), lambda at: (0, at)),
            pl.BlockSpec((2, seq_rows), lambda at: (0, 0)),
            pl.BlockSpec((seq_rows, 2), lambda at: (0, 0)),
        ],
        out_specs=pl.BlockSpec((2, seq_rows, seq_rows), lambda at: (at, 0, 0)),
        out_shape=jax.ShapeDtypeStruct((width // DH, seq_rows, seq_rows), BF16),
        compiler_params=pltpu.CompilerParams(vmem_limit_bytes=40 << 20),
        cost_estimate=pl.CostEstimate(
            flops=2 * width * seq_rows * seq_rows,
            transcendentals=width // DH * seq_rows * seq_rows,
            bytes_accessed=width // DH * seq_rows * seq_rows * 2,
        ),
    )(query_rows, key_rows, by_query, by_query.T)


def attention_body(attend_ref, query_ref, key_ref, value_ref, heads_ref, grad_ref, out_ref):
    width = query_ref.shape[1]
    products = grad_ref[...].astype(F32) * heads_ref[...].astype(F32)
    products = products.T
    for head in range(width // DH):
        cols = slice(head * DH, head * DH + DH)
        row_dot = jnp.sum(products[cols], axis=0, keepdims=True)
        attend = attend_ref[head]
        grads = grad_ref[:, cols]
        attend_grad = contract_last(value_ref[:, cols], grads)
        score_grad = attend.astype(F32) * (attend_grad - row_dot) * (DH ** (-0.5))
        score_grad = score_grad.astype(BF16)
        for at, back in enumerate(
            (
                contract_first(score_grad, key_ref[:, cols]),
                jnp.dot(score_grad, query_ref[:, cols], preferred_element_type=F32),
                jnp.dot(attend, grads, preferred_element_type=F32),
            )
        ):
            low = at * width + head * DH
            out_ref[:, low : low + DH] = back.astype(BF16)


def attention_back(attend, query_rows, key_rows, value_rows, attn_heads, head_grad, pair_at):
    seq_rows = query_rows.shape[0]
    pair = 2 * DH
    cols = pl.BlockSpec((seq_rows, pair), lambda at: (0, pair_at))
    return pl.pallas_call(
        attention_body,
        grid=(1,),
        in_specs=[
            pl.BlockSpec((2, seq_rows, seq_rows), lambda at: (pair_at, 0, 0)),
            cols,
            cols,
            cols,
            cols,
            cols,
        ],
        out_specs=pl.BlockSpec((seq_rows, 3 * pair), lambda at: (0, 0)),
        out_shape=jax.ShapeDtypeStruct((seq_rows, 3 * pair), BF16),
        compiler_params=pltpu.CompilerParams(vmem_limit_bytes=40 << 20),
        cost_estimate=pl.CostEstimate(
            flops=8 * pair * seq_rows * seq_rows,
            transcendentals=0,
            bytes_accessed=4 * seq_rows * seq_rows + 16 * pair * seq_rows,
        ),
    )(attend, query_rows, key_rows, value_rows, attn_heads, head_grad)


def shards(
    layer_input,
    residual,
    out_grad,
    gate_prob,
    expert_ids,
    slot_index,
    segment_ids,
    query_rows,
    key_rows,
    value_rows,
    attn_heads,
    attn_gain,
    expert_gain,
    query_weight,
    key_weight,
    value_weight,
    output_weight,
    inner_weight,
    outer_weight,
    hidden_pre,
):
    tensor_count = lax.axis_size("tensor")
    expert_count = lax.axis_size("expert")
    tensor_at = lax.axis_index("tensor")
    expert_at = lax.axis_index("expert")
    tok_rows, model_width = layer_input.shape
    slot_count = hidden_pre.shape[3]
    unit_count = hidden_pre.shape[4]
    slot_pad = -(-slot_count // 8) * 8
    group_rows = expert_count * slot_pad

    tensor_bits = list(range(bits_of("tensor")))
    expert_bits = list(range(bits_of("expert")))

    inv_mid = inv_rms(residual)
    normed_mid = (residual.astype(F32) * inv_mid * expert_gain).astype(BF16)
    scaled_grad = (gate_prob[:, None] * out_grad.astype(F32)).astype(BF16)

    def placing_of(experts):
        target = jnp.where(slot_index >= 0, experts * slot_pad + slot_index, -1)
        places = jnp.arange(group_rows, dtype=jnp.int32)
        return (places[:, None] == target[None, :]).astype(BF16)

    def by_expert(rows):
        return rows.reshape(expert_count, slot_pad, -1)

    placing = placing_of(expert_ids)
    send_grads = jnp.dot(placing, scaled_grad, preferred_element_type=F32).astype(BF16)
    send_rows = jnp.dot(placing, normed_mid, preferred_element_type=F32).astype(BF16)
    got_grads = exchange(by_expert(send_grads), "expert").reshape(group_rows, model_width)
    grad_blocks = gather_rel(got_grads, "tensor")
    input_blocks = gather_rel(layer_input, "tensor")
    send_rows, _ = lax.optimization_barrier((send_rows, got_grads))
    got_rows = exchange(by_expert(send_rows), "expert").reshape(group_rows, model_width)

    pre_blocks = []
    for shard_block in pick_rel(hidden_pre[0], tensor_at, tensor_count):
        block = jnp.pad(shard_block, ((0, 0), (0, slot_pad - slot_count), (0, 0)))
        pre_blocks.append(block.reshape(group_rows, unit_count))

    parts, pre_grads = [], []
    for grads, pre in zip(grad_blocks, pre_blocks):
        up_grad = contract_last(grads, outer_weight[0])
        pre_grad = jnp.where(pre > 0, up_grad, 0.0).astype(BF16)
        gate_part = jnp.sum(jnp.maximum(pre, 0).astype(F32) * up_grad, axis=1, keepdims=True)
        slot_part = contract_last(pre_grad, inner_weight[0])
        parts.append(jnp.concatenate([slot_part.astype(BF16), gate_part.astype(BF16)], axis=1))
        pre_grads.append(pre_grad)
    slot_sum = scatter_sum_rel(parts, "tensor", tensor_bits).astype(BF16)
    back_parts = pick_rel(by_expert(slot_sum), expert_at, expert_count)
    back_flat = jnp.concatenate(exchange_rel(back_parts, "expert"), axis=0)

    token_back = contract_first(placing_of(expert_ids ^ expert_at), back_flat)
    mid_grad = token_back[:, :model_width]
    gate_grad = token_back[:, model_width].astype(BF16)
    wide_residual = residual.astype(F32)
    gain_mid = jnp.sum(mid_grad * wide_residual * inv_mid, axis=0)
    resid_grad = out_grad.astype(F32) + norm_back(mid_grad, residual, inv_mid, expert_gain)
    resid_low = resid_grad.astype(BF16)

    seq_order = halving_order(tensor_bits)
    resid_blocks = gather_rel(resid_low, "tensor")
    piece = jnp.concatenate([resid_blocks[rel] for rel in seq_order], axis=0)

    def seq_rel(rows):
        blocks = rows.reshape((tensor_count, tok_rows) + rows.shape[1:])
        picked = pick_rel(blocks, tensor_at, tensor_count)
        return jnp.concatenate([picked[rel] for rel in seq_order], axis=0)

    query_rel, key_rel, value_rel, heads_rel, segments, positions = (
        seq_rel(rows)
        for rows in (
            query_rows,
            key_rows,
            value_rows,
            attn_heads,
            segment_ids,
            jnp.arange(tensor_count * tok_rows, dtype=jnp.int32),
        )
    )
    attend = softmax_transposed(query_rel, key_rel, positions, segments)

    share_rows = model_width // expert_count
    share_pad = -(-share_rows // 8) * 8

    def shares_of(rows, order):
        blocks = [
            jnp.pad(
                lax.dynamic_slice_in_dim(rows, (expert_at ^ rel) * share_rows, share_rows, 0),
                ((0, share_pad - share_rows), (0, 0)),
            )
            for rel in halving_order(order)
        ]
        return jnp.concatenate(blocks, axis=0)

    barrier = lax.optimization_barrier
    input_seq = jnp.concatenate([input_blocks[rel] for rel in seq_order], axis=0)
    input_seq, _ = barrier((input_seq, parts[-1]))
    unit_seq = input_seq.astype(F32) * inv_rms(input_seq)
    normed_cols = (unit_seq * attn_gain).astype(BF16).T
    pair_orders = [expert_bits, expert_bits[1:2] + expert_bits[:1] + expert_bits[2:]]
    pair_shares = [shares_of(normed_cols, order) for order in pair_orders]
    piece, pair_shares = barrier((piece, pair_shares))

    head_grad = contract_last(piece, output_weight).astype(BF16)
    pair = 2 * DH
    backs, shares, normed_parts = [], [], 0.0
    for at in range(query_rows.shape[1] // pair):
        back_cols = attention_back(attend, query_rel, key_rel, value_rel, heads_rel, head_grad, at)
        which = at % len(pair_orders)
        shares.append(
            jnp.dot(pair_shares[which], back_cols, preferred_element_type=F32).astype(BF16)
        )
        backs.append(back_cols)
    backs, shares, got_rows = barrier((backs, shares, got_rows))
    orders = [pair_orders[at % len(pair_orders)] for at in range(len(shares))]

    def next_sums(sums, step, other):
        halves = [part.shape[0] // 2 for part in sums]
        got = [
            flip(part[half:].astype(BF16), "expert", 1 << order[step])
            for part, half, order in zip(sums, halves, orders)
        ]
        got, other = barrier((got, other))
        sums = [part[:half].astype(F32) + block.astype(F32) for part, half, block in zip(sums, halves, got)]
        if step < len(expert_bits) - 1:
            sums = [part.astype(BF16) for part in sums]
        return sums, other

    sums, piece = next_sums(shares, 0, piece)
    for at, back_cols in enumerate(backs):
        for index, weight in enumerate((query_weight, key_weight, value_weight)):
            normed_parts = normed_parts + contract_last(
                back_cols[:, index * pair : (index + 1) * pair],
                weight[:, at * pair : (at + 1) * pair],
            )
    normed_grad = halve_sum(normed_parts.astype(BF16), "tensor", tensor_bits)
    gains = jnp.stack([jnp.sum(normed_parts * unit_seq, axis=0), gain_mid])

    sums, piece = barrier((sums, piece))
    flat_rows = jnp.concatenate(gather_rel(got_rows, "tensor"), axis=0)
    active = jnp.maximum(jnp.concatenate(pre_blocks, axis=0), 0)
    inner_grad = contract_first(flat_rows, jnp.concatenate(pre_grads, axis=0)).astype(BF16)[None]

    out_sum = contract_first(piece, heads_rel).astype(BF16)
    out_shares = shares_of(out_sum, expert_bits)

    if len(expert_bits) > 1:
        sums, out_shares = next_sums(sums, 1, out_shares)
    sums, out_shares, gains = barrier((sums, out_shares, gains))
    for bit in tensor_bits:
        gains = gains + flip(gains, "tensor", 1 << bit)
    out_half = out_shares.shape[0] // 2
    out_got = flip(out_shares[out_half:], "expert", 1 << expert_bits[0])
    for step in range(2, len(expert_bits)):
        sums, out_got = next_sums(sums, step, out_got)
    out_part = (out_shares[:out_half].astype(F32) + out_got.astype(F32)).astype(BF16)
    sums, out_part, gains = barrier((sums, out_part, gains))
    gains = gains + flip(gains, "expert", 1)
    inv_in = inv_rms(layer_input)
    input_grad = (resid_grad + norm_back(normed_grad, layer_input, inv_in, attn_gain)).astype(BF16)
    for step in range(1, len(expert_bits)):
        if step == len(expert_bits) - 1:
            out_part, inner_grad, input_grad, grad_blocks, gains = barrier(
                (out_part, inner_grad, input_grad, grad_blocks, gains)
            )
            for bit in expert_bits[1:]:
                gains = gains + flip(gains, "expert", 1 << bit)
        out_part = halve_sum(out_part.astype(BF16), "expert", [expert_bits[step]])
    out_part = out_part[:share_rows]
    weight_sums = [part[:share_rows] for part in sums]
    flat_grads = jnp.concatenate(grad_blocks, axis=0)
    outer_grad = contract_first(active, flat_grads).astype(BF16)[None]
    query_part, key_part, value_part = (
        jnp.concatenate(
            [total[:, index * pair : (index + 1) * pair] for total in weight_sums], axis=1
        ).astype(BF16)
        for index in range(3)
    )

    return (
        input_grad,
        gains[0],
        gains[1],
        query_part,
        key_part,
        value_part,
        out_part.astype(BF16).T,
        inner_grad,
        outer_grad,
        gate_grad,
    )


def solution(mesh):
    return jax.shard_map(
        shards,
        mesh=mesh,
        in_specs=(
            P(("expert", "tensor"), None),
            P(("expert", "tensor"), None),
            P(("expert", "tensor"), None),
            P(("expert", "tensor")),
            P(("expert", "tensor")),
            P(("expert", "tensor")),
            P("expert"),
            P("expert", "tensor"),
            P("expert", "tensor"),
            P("expert", "tensor"),
            P("expert", "tensor"),
            P(),
            P(),
            P(None, "tensor"),
            P(None, "tensor"),
            P(None, "tensor"),
            P("tensor", None),
            P("expert", None, "tensor"),
            P("expert", "tensor", None),
            P("expert", None, None, None, "tensor"),
        ),
        out_specs=(
            P(("expert", "tensor"), None),
            P(),
            P(),
            P("expert", "tensor"),
            P("expert", "tensor"),
            P("expert", "tensor"),
            P("tensor", "expert"),
            P("expert", None, "tensor"),
            P("expert", "tensor", None),
            P(("expert", "tensor")),
        ),
        check_vma=False,
    )
```

```python
import jax
import jax.numpy as jnp
from jax import lax
from jax.experimental import pallas as pl
from jax.experimental.pallas import tpu as pltpu
from jax.sharding import PartitionSpec as P

DH = 64


EPS = 1e-06

F32 = jnp.float32
BF16 = jnp.bfloat16

MOST_PERMUTES = 8


def inv_rms(row_data):
    wide_rows = row_data.astype(F32)
    return lax.rsqrt(jnp.mean(wide_rows * wide_rows, axis=-1, keepdims=True) + EPS)


def norm_back(grad_rows, row_data, inv_rows, gain_row):
    wide_rows = row_data.astype(F32)
    scaled = grad_rows * gain_row
    return inv_rows * (
        scaled
        - wide_rows * inv_rows * inv_rows * jnp.mean(scaled * wide_rows, axis=-1, keepdims=True)
    )


def contract_last(left, right):
    return lax.dot_general(left, right, (((1,), (1,)), ((), ())), preferred_element_type=F32)


def contract_first(left, right):
    return lax.dot_general(left, right, (((0,), (0,)), ((), ())), preferred_element_type=F32)


def flip(value, axis, mask):
    count = lax.axis_size(axis)
    return lax.ppermute(value, axis, [(at, at ^ mask) for at in range(count)])


def bits_of(axis):
    return lax.axis_size(axis).bit_length() - 1


def gather_rel(value, axis):
    held = {0: value}
    for bit in reversed(range(bits_of(axis))):
        for rel in list(held):
            held[rel | (1 << bit)] = flip(held[rel], axis, 1 << bit)
    return [held[rel] for rel in range(len(held))]


def pick_rel(blocks, index, count):
    return [lax.dynamic_index_in_dim(blocks, index ^ rel, 0, keepdims=False) for rel in range(count)]


def scatter_sum_rel(parts, axis, order):
    if len(parts) > MOST_PERMUTES:
        whole = jnp.stack(pick_rel(jnp.stack(parts), lax.axis_index(axis), len(parts)))
        return lax.psum_scatter(whole, axis, scatter_dimension=0, tiled=False).astype(F32)
    held = dict(enumerate(parts))
    for step, bit in enumerate(order):
        mask = 1 << bit
        last = step == len(order) - 1
        for rel in [r for r in held if r & mask]:
            got = flip(held.pop(rel), axis, mask)
            total = held[rel ^ mask].astype(F32) + got.astype(F32)
            held[rel ^ mask] = total if last else total.astype(BF16)
    return held[0]


def exchange_rel(parts, axis):
    count = len(parts)
    if count > MOST_PERMUTES:
        whole = jnp.stack(pick_rel(jnp.stack(parts), lax.axis_index(axis), count))
        whole = lax.all_to_all(whole, axis, split_axis=0, concat_axis=0, tiled=True)
        return pick_rel(whole, lax.axis_index(axis), count)
    got = {0: parts[0]}
    for rel in reversed(range(1, count)):
        got[rel] = flip(parts[rel], axis, rel)
    return [got[rel] for rel in range(count)]


def halving_order(order):
    places = 1 << len(order)
    last = len(order) - 1
    return [
        sum(((place >> (last - at)) & 1) << bit for at, bit in enumerate(order))
        for place in range(places)
    ]


def halve_sum(shares, axis, order):
    for step, bit in enumerate(order):
        half = shares.shape[0] // 2
        got = flip(shares[half:], axis, 1 << bit)
        shares = shares[:half].astype(F32) + got.astype(F32)
        if step < len(order) - 1:
            shares = shares.astype(BF16)
    return shares


def exchange(blocks, axis):
    return lax.all_to_all(blocks, axis, split_axis=0, concat_axis=0, tiled=True)


def softmax_body(query_ref, key_ref, row_ref, col_ref, out_ref):
    position_q, segment_q = row_ref[0:1, :], row_ref[1:2, :]
    position_k, segment_k = col_ref[:, 0:1], col_ref[:, 1:2]
    allowed = (position_q >= position_k) & (segment_q == segment_k)
    for head in range(query_ref.shape[1] // DH):
        cols = slice(head * DH, head * DH + DH)
        scores = contract_last(key_ref[:, cols], query_ref[:, cols]) * (DH ** (-0.5))
        scores = jnp.where(allowed, scores, -jnp.inf)
        weights = jnp.exp(scores - jnp.max(scores, axis=0, keepdims=True))
        attend = weights / jnp.sum(weights, axis=0, keepdims=True)
        out_ref[head] = attend.astype(BF16)


def softmax_transposed(query_rows, key_rows, positions, segments):
    seq_rows, width = query_rows.shape
    pair = 2 * DH
    by_query = jnp.stack([positions, segments])
    return pl.pallas_call(
        softmax_body,
        grid=(width // pair,),
        in_specs=[
            pl.BlockSpec((seq_rows, pair), lambda at: (0, at)),
            pl.BlockSpec((seq_rows, pair), lambda at: (0, at)),
            pl.BlockSpec((2, seq_rows), lambda at: (0, 0)),
            pl.BlockSpec((seq_rows, 2), lambda at: (0, 0)),
        ],
        out_specs=pl.BlockSpec((2, seq_rows, seq_rows), lambda at: (at, 0, 0)),
        out_shape=jax.ShapeDtypeStruct((width // DH, seq_rows, seq_rows), BF16),
        compiler_params=pltpu.CompilerParams(vmem_limit_bytes=40 << 20),
        cost_estimate=pl.CostEstimate(
            flops=2 * width * seq_rows * seq_rows,
            transcendentals=width // DH * seq_rows * seq_rows,
            bytes_accessed=width // DH * seq_rows * seq_rows * 2,
        ),
    )(query_rows, key_rows, by_query, by_query.T)


def attention_body(attend_ref, query_ref, key_ref, value_ref, heads_ref, grad_ref, out_ref):
    width = query_ref.shape[1]
    products = grad_ref[...].astype(F32) * heads_ref[...].astype(F32)
    products = products.T
    for head in range(width // DH):
        cols = slice(head * DH, head * DH + DH)
        row_dot = jnp.sum(products[cols], axis=0, keepdims=True)
        attend = attend_ref[head]
        grads = grad_ref[:, cols]
        attend_grad = contract_last(value_ref[:, cols], grads)
        score_grad = attend.astype(F32) * (attend_grad - row_dot) * (DH ** (-0.5))
        score_grad = score_grad.astype(BF16)
        for at, back in enumerate(
            (
                contract_first(score_grad, key_ref[:, cols]),
                jnp.dot(score_grad, query_ref[:, cols], preferred_element_type=F32),
                jnp.dot(attend, grads, preferred_element_type=F32),
            )
        ):
            low = at * width + head * DH
            out_ref[:, low : low + DH] = back.astype(BF16)


def attention_back(attend, query_rows, key_rows, value_rows, attn_heads, head_grad, pair_at):
    seq_rows = query_rows.shape[0]
    pair = 2 * DH
    cols = pl.BlockSpec((seq_rows, pair), lambda at: (0, pair_at))
    return pl.pallas_call(
        attention_body,
        grid=(1,),
        in_specs=[
            pl.BlockSpec((2, seq_rows, seq_rows), lambda at: (pair_at, 0, 0)),
            cols,
            cols,
            cols,
            cols,
            cols,
        ],
        out_specs=pl.BlockSpec((seq_rows, 3 * pair), lambda at: (0, 0)),
        out_shape=jax.ShapeDtypeStruct((seq_rows, 3 * pair), BF16),
        compiler_params=pltpu.CompilerParams(vmem_limit_bytes=40 << 20),
        cost_estimate=pl.CostEstimate(
            flops=8 * pair * seq_rows * seq_rows,
            transcendentals=0,
            bytes_accessed=4 * seq_rows * seq_rows + 16 * pair * seq_rows,
        ),
    )(attend, query_rows, key_rows, value_rows, attn_heads, head_grad)


def shards(
    layer_input,
    residual,
    out_grad,
    gate_prob,
    expert_ids,
    slot_index,
    segment_ids,
    query_rows,
    key_rows,
    value_rows,
    attn_heads,
    attn_gain,
    expert_gain,
    query_weight,
    key_weight,
    value_weight,
    output_weight,
    inner_weight,
    outer_weight,
    hidden_pre,
):
    tensor_count = lax.axis_size("tensor")
    expert_count = lax.axis_size("expert")
    tensor_at = lax.axis_index("tensor")
    expert_at = lax.axis_index("expert")
    tok_rows, model_width = layer_input.shape
    slot_count = hidden_pre.shape[3]
    unit_count = hidden_pre.shape[4]
    slot_pad = -(-slot_count // 8) * 8
    group_rows = expert_count * slot_pad

    tensor_bits = list(range(bits_of("tensor")))
    expert_bits = list(range(bits_of("expert")))

    inv_mid = inv_rms(residual)
    normed_mid = (residual.astype(F32) * inv_mid * expert_gain).astype(BF16)
    scaled_grad = (gate_prob[:, None] * out_grad.astype(F32)).astype(BF16)

    def placing_of(experts):
        target = jnp.where(slot_index >= 0, experts * slot_pad + slot_index, -1)
        places = jnp.arange(group_rows, dtype=jnp.int32)
        return (places[:, None] == target[None, :]).astype(BF16)

    def by_expert(rows):
        return rows.reshape(expert_count, slot_pad, -1)

    placing = placing_of(expert_ids)
    send_grads = jnp.dot(placing, scaled_grad, preferred_element_type=F32).astype(BF16)
    send_rows = jnp.dot(placing, normed_mid, preferred_element_type=F32).astype(BF16)
    got_grads = exchange(by_expert(send_grads), "expert").reshape(group_rows, model_width)
    grad_blocks = gather_rel(got_grads, "tensor")
    input_blocks = gather_rel(layer_input, "tensor")
    send_rows, _ = lax.optimization_barrier((send_rows, got_grads))
    got_rows = exchange(by_expert(send_rows), "expert").reshape(group_rows, model_width)

    pre_blocks = []
    for shard_block in pick_rel(hidden_pre[0], tensor_at, tensor_count):
        block = jnp.pad(shard_block, ((0, 0), (0, slot_pad - slot_count), (0, 0)))
        pre_blocks.append(block.reshape(group_rows, unit_count))

    parts, pre_grads = [], []
    for grads, pre in zip(grad_blocks, pre_blocks):
        up_grad = contract_last(grads, outer_weight[0])
        pre_grad = jnp.where(pre > 0, up_grad, 0.0).astype(BF16)
        gate_part = jnp.sum(jnp.maximum(pre, 0).astype(F32) * up_grad, axis=1, keepdims=True)
        slot_part = contract_last(pre_grad, inner_weight[0])
        parts.append(jnp.concatenate([slot_part.astype(BF16), gate_part.astype(BF16)], axis=1))
        pre_grads.append(pre_grad)
    slot_sum = scatter_sum_rel(parts, "tensor", tensor_bits).astype(BF16)
    back_parts = pick_rel(by_expert(slot_sum), expert_at, expert_count)
    back_flat = jnp.concatenate(exchange_rel(back_parts, "expert"), axis=0)

    token_back = contract_first(placing_of(expert_ids ^ expert_at), back_flat)
    mid_grad = token_back[:, :model_width]
    gate_grad = token_back[:, model_width].astype(BF16)
    wide_residual = residual.astype(F32)
    gain_mid = jnp.sum(mid_grad * wide_residual * inv_mid, axis=0)
    resid_grad = out_grad.astype(F32) + norm_back(mid_grad, residual, inv_mid, expert_gain)
    resid_low = resid_grad.astype(BF16)

    seq_order = halving_order(tensor_bits)
    resid_blocks = gather_rel(resid_low, "tensor")
    piece = jnp.concatenate([resid_blocks[rel] for rel in seq_order], axis=0)

    def seq_rel(rows):
        blocks = rows.reshape((tensor_count, tok_rows) + rows.shape[1:])
        picked = pick_rel(blocks, tensor_at, tensor_count)
        return jnp.concatenate([picked[rel] for rel in seq_order], axis=0)

    query_rel, key_rel, value_rel, heads_rel, segments, positions = (
        seq_rel(rows)
        for rows in (
            query_rows,
            key_rows,
            value_rows,
            attn_heads,
            segment_ids,
            jnp.arange(tensor_count * tok_rows, dtype=jnp.int32),
        )
    )
    attend = softmax_transposed(query_rel, key_rel, positions, segments)

    share_rows = model_width // expert_count
    share_pad = -(-share_rows // 8) * 8

    def shares_of(rows, order):
        blocks = [
            jnp.pad(
                lax.dynamic_slice_in_dim(rows, (expert_at ^ rel) * share_rows, share_rows, 0),
                ((0, share_pad - share_rows), (0, 0)),
            )
            for rel in halving_order(order)
        ]
        return jnp.concatenate(blocks, axis=0)

    barrier = lax.optimization_barrier
    input_seq = jnp.concatenate([input_blocks[rel] for rel in seq_order], axis=0)
    input_seq, _ = barrier((input_seq, parts[-1]))
    unit_seq = input_seq.astype(F32) * inv_rms(input_seq)
    normed_cols = (unit_seq * attn_gain).astype(BF16).T
    pair_orders = [expert_bits, expert_bits[1:2] + expert_bits[:1] + expert_bits[2:]]
    pair_shares = [shares_of(normed_cols, order) for order in pair_orders]
    piece, pair_shares = barrier((piece, pair_shares))

    head_grad = contract_last(piece, output_weight).astype(BF16)
    pair = 2 * DH
    backs, shares, normed_parts = [], [], 0.0
    for at in range(query_rows.shape[1] // pair):
        back_cols = attention_back(attend, query_rel, key_rel, value_rel, heads_rel, head_grad, at)
        which = at % len(pair_orders)
        shares.append(
            jnp.dot(pair_shares[which], back_cols, preferred_element_type=F32).astype(BF16)
        )
        backs.append(back_cols)
    backs, _, got_rows = barrier((backs, shares, got_rows))
    orders = [pair_orders[at % len(pair_orders)] for at in range(len(shares))]

    def next_sums(sums, step, other):
        halves = [part.shape[0] // 2 for part in sums]
        got = [
            flip(part[half:].astype(BF16), "expert", 1 << order[step])
            for part, half, order in zip(sums, halves, orders)
        ]
        got, other = barrier((got, other))
        sums = [part[:half].astype(F32) + block.astype(F32) for part, half, block in zip(sums, halves, got)]
        if step < len(expert_bits) - 1:
            sums = [part.astype(BF16) for part in sums]
        return sums, other

    sums, piece = next_sums(shares, 0, piece)
    for at, back_cols in enumerate(backs):
        for index, weight in enumerate((query_weight, key_weight, value_weight)):
            normed_parts = normed_parts + contract_last(
                back_cols[:, index * pair : (index + 1) * pair],
                weight[:, at * pair : (at + 1) * pair],
            )
    normed_grad = halve_sum(normed_parts.astype(BF16), "tensor", tensor_bits)
    gains = jnp.stack([jnp.sum(normed_parts * unit_seq, axis=0), gain_mid])

    sums, piece = barrier((sums, piece))
    flat_rows = jnp.concatenate(gather_rel(got_rows, "tensor"), axis=0)
    active = jnp.maximum(jnp.concatenate(pre_blocks, axis=0), 0)
    inner_grad = contract_first(flat_rows, jnp.concatenate(pre_grads, axis=0)).astype(BF16)[None]

    out_sum = contract_first(piece, heads_rel).astype(BF16)
    out_shares = shares_of(out_sum, expert_bits)

    if len(expert_bits) > 1:
        sums, out_shares = next_sums(sums, 1, out_shares)
    sums, out_shares, gains = barrier((sums, out_shares, gains))
    for bit in tensor_bits:
        gains = gains + flip(gains, "tensor", 1 << bit)
    out_half = out_shares.shape[0] // 2
    out_got = flip(out_shares[out_half:], "expert", 1 << expert_bits[0])
    for step in range(2, len(expert_bits)):
        sums, out_got = next_sums(sums, step, out_got)
    out_part = (out_shares[:out_half].astype(F32) + out_got.astype(F32)).astype(BF16)
    sums, out_part, gains = barrier((sums, out_part, gains))
    out_part, grad_blocks = barrier((out_part, grad_blocks))
    flat_grads = jnp.concatenate(grad_blocks, axis=0)
    outer_grad = contract_first(active, flat_grads).astype(BF16)[None]
    gains = gains + flip(gains, "expert", 1)
    inv_in = inv_rms(layer_input)
    input_grad = (resid_grad + norm_back(normed_grad, layer_input, inv_in, attn_gain)).astype(BF16)
    for step in range(1, len(expert_bits)):
        if step == len(expert_bits) - 1:
            out_part, inner_grad, input_grad, gains, outer_grad = barrier(
                (out_part, inner_grad, input_grad, gains, outer_grad)
            )
            for bit in expert_bits[1:]:
                gains = gains + flip(gains, "expert", 1 << bit)
        out_part = halve_sum(out_part.astype(BF16), "expert", [expert_bits[step]])
    out_part = out_part[:share_rows]
    weight_sums = [part[:share_rows] for part in sums]
    query_part, key_part, value_part = (
        jnp.concatenate(
            [total[:, index * pair : (index + 1) * pair] for total in weight_sums], axis=1
        ).astype(BF16)
        for index in range(3)
    )

    return (
        input_grad,
        gains[0],
        gains[1],
        query_part,
        key_part,
        value_part,
        out_part.astype(BF16).T,
        inner_grad,
        outer_grad,
        gate_grad,
    )


def solution(mesh):
    return jax.shard_map(
        shards,
        mesh=mesh,
        in_specs=(
            P(("expert", "tensor"), None),
            P(("expert", "tensor"), None),
            P(("expert", "tensor"), None),
            P(("expert", "tensor")),
            P(("expert", "tensor")),
            P(("expert", "tensor")),
            P("expert"),
            P("expert", "tensor"),
            P("expert", "tensor"),
            P("expert", "tensor"),
            P("expert", "tensor"),
            P(),
            P(),
            P(None, "tensor"),
            P(None, "tensor"),
            P(None, "tensor"),
            P("tensor", None),
            P("expert", None, "tensor"),
            P("expert", "tensor", None),
            P("expert", None, None, None, "tensor"),
        ),
        out_specs=(
            P(("expert", "tensor"), None),
            P(),
            P(),
            P("expert", "tensor"),
            P("expert", "tensor"),
            P("expert", "tensor"),
            P("tensor", "expert"),
            P("expert", None, "tensor"),
            P("expert", "tensor", None),
            P(("expert", "tensor")),
        ),
        check_vma=False,
    )
```
